512 devices in a mesh: head: 16 (over y_lo, x, core), gx: 32 (over y_hi, z).
Axes of the slice: x: 4, y: 4 (y_hi: 2, y_lo: 2; y = y_hi * 2 + y_lo), z: 16, core: 2. Of those that a mesh axis runs over, the one named last changes fastest.
Arguments:
- level_set: float32 [288, 192, 8, 128], P('gx', 'head'), may hold values from -6 to 6
- wind_field: float32 [2, 288, 128], P(None, 'gx'), may hold values from -3 to 3
- target_mask: int32 [288, 128], P('gx'), may hold values 0 or 1
- target_depth: float32 [288, 128], P('gx'), may hold values from 0.2 to 2
Outputs:
- level_next: float32 [288, 192, 8, 128], P('gx', 'head')
The draws below stay inside these ranges and needn't reach their ends.
Inputs may be any that keep to these rules, and one draw needn't show every extreme that they name: `target_mask`: 1 marks a cell of the target set, 0 a cell outside it.
All inputs are finite; a program needn't handle non-finite values. No bound on the sum of `target_mask` on one device may be relied on, other than what follows from the above.
Results may differ from the reference program's by a relative error of at most 0.0003.
Values sent between devices are 32-bit elements; how exact they have to be, the bound alone decides.
A program may use at most 64 MiB of HBM per device.

```python
import math
import jax
import jax.numpy as jnp
from jax import lax

NV = 8
NY = 128
NX = 288
NTH = 192


def with_ends(result, stream_key, low, high):
    spot = [jax.random.randint(jax.random.fold_in(stream_key, axis), (), 0, length) for axis, length in enumerate(result.shape)]
    widest = result.shape.index(max(result.shape))
    neighbour = spot[:widest] + [(spot[widest] + 1) % result.shape[widest]] + spot[widest + 1:]
    return result.at[tuple(spot)].set(low).at[tuple(neighbour)].set(high)


def block_scale(own_key, extent, cuts, low, top_value):
    gain, own = 1.0, jax.random.fold_in(own_key, 6)
    for dim, parts in cuts:
        steps = jnp.exp(jax.random.uniform(jax.random.fold_in(own, dim), (parts,), jnp.float32, low / len(cuts), top_value / len(cuts)))
        gain = gain * jnp.repeat(steps, extent[dim] // parts).reshape([-1 if axis == dim else 1 for axis in range(len(extent))])
    return gain


def centred(own_key, shape, deviation, bound, pieces=(), kind=jnp.bfloat16):
    gain = block_scale(own_key, shape, pieces, -0.22, 0.18) if pieces else 1.0
    drawn = jax.random.normal(own_key, shape, jnp.float32) * deviation * gain
    return jnp.minimum(jnp.maximum(drawn, -bound), bound).astype(kind)


def setup_inputs(seed: int = 0) -> dict:
    seeds = jax.random.split(jax.random.key(seed), 5)
    level_set = centred(seeds[0], (NX, NTH, NV, NY), 1.0, 6.0, ((0, 32), (1, 16)), jnp.float32)
    wind_field = centred(seeds[1], (2, NX, NY), 0.5, 3.0, ((1, 32),), jnp.float32)
    target_mask = with_ends((jax.random.randint(seeds[2], (NX, NY), 0, 3) < 1).astype(jnp.int32), jax.random.fold_in(seeds[2], 1), 0, 1)
    target_depth = jnp.clip(jnp.exp(math.log(2.0) - 2.3025851 * jax.random.uniform(seeds[3], (NX, NY), jnp.float32) ** block_scale(seeds[3], (NX, NY), ((0, 32),), -0.2, 0.2)), 0.2, 2.0)
    return {"level_set": level_set, "wind_field": wind_field, "target_mask": target_mask, "target_depth": target_depth}


epsilon = 1e-6
courant = 0.5
spacing = 0.05
turn_limit = 1.0
thrust_limit = 0.5
speed_low = 0.5
speed_high = 1.5


def weno_side(slope_a, slope_b, slope_c, slope_d, slope_e):
    guess_a = slope_a / 3.0 - 7.0 * slope_b / 6.0 + 11.0 * slope_c / 6.0
    guess_b = -slope_b / 6.0 + 5.0 * slope_c / 6.0 + slope_d / 3.0
    guess_c = slope_c / 3.0 + 5.0 * slope_d / 6.0 - slope_e / 6.0
    bend_a = slope_a - 2.0 * slope_b + slope_c
    tilt_a = slope_a - 4.0 * slope_b + 3.0 * slope_c
    bend_b = slope_b - 2.0 * slope_c + slope_d
    tilt_b = slope_b - slope_d
    bend_c = slope_c - 2.0 * slope_d + slope_e
    tilt_c = 3.0 * slope_c - 4.0 * slope_d + slope_e
    smooth_a = 13.0 / 12.0 * bend_a * bend_a + 0.25 * tilt_a * tilt_a + epsilon
    smooth_b = 13.0 / 12.0 * bend_b * bend_b + 0.25 * tilt_b * tilt_b + epsilon
    smooth_c = 13.0 / 12.0 * bend_c * bend_c + 0.25 * tilt_c * tilt_c + epsilon
    weight_a = 0.1 / (smooth_a * smooth_a)
    weight_b = 0.6 / (smooth_b * smooth_b)
    weight_c = 0.3 / (smooth_c * smooth_c)
    return (weight_a * guess_a + weight_b * guess_b + weight_c * guess_c) / (weight_a + weight_b + weight_c)


def weno_pair(padded, along, step_size):
    inner_count = padded.shape[along] - 6
    differences = jnp.diff(padded, axis=along) / step_size

    def window(offset):
        return lax.slice_in_dim(differences, offset, offset + inner_count, axis=along)

    minus_side = weno_side(window(0), window(1), window(2), window(3), window(4))
    plus_side = weno_side(window(5), window(4), window(3), window(2), window(1))
    return minus_side, plus_side


def hamilton(padded, heading_step, speed_step, speeds, cosines, sines, wind_x, wind_y, peak_x, peak_y):
    inner = padded[3:-3, 3:-3]
    minus_x, plus_x = weno_pair(padded[:, 3:-3], 0, spacing)
    minus_t, plus_t = weno_pair(padded[3:-3], 1, heading_step)
    minus_v, plus_v = weno_pair(jnp.pad(inner, ((0, 0), (0, 0), (3, 3), (0, 0)), mode="edge"), 2, speed_step)
    minus_y, plus_y = weno_pair(jnp.pad(inner, ((0, 0), (0, 0), (0, 0), (3, 3)), mode="edge"), 3, spacing)
    flow_x = speeds * cosines + wind_x
    flow_y = speeds * sines + wind_y
    slope_x = 0.5 * (minus_x + plus_x)
    slope_y = 0.5 * (minus_y + plus_y)
    slope_t = 0.5 * (minus_t + plus_t)
    slope_v = 0.5 * (minus_v + plus_v)
    drift = slope_x * flow_x + slope_y * flow_y - turn_limit * jnp.abs(slope_t) - thrust_limit * jnp.abs(slope_v)
    spread = peak_x * (plus_x - minus_x) + peak_y * (plus_y - minus_y) + turn_limit * (plus_t - minus_t) + thrust_limit * (plus_v - minus_v)
    return drift + 0.5 * spread


def reference(level_set, wind_field, target_mask, target_depth):
    heading_step = 2.0 * math.pi / NTH
    speed_step = (speed_high - speed_low) / (NV - 1)
    speed_row = speed_low + jnp.arange(NV, dtype=jnp.int32).astype(jnp.float32) * speed_step
    angles = jnp.arange(NTH, dtype=jnp.int32).astype(jnp.float32) * heading_step
    cosine_row = jnp.cos(angles)
    sine_row = jnp.sin(angles)
    wind_x = wind_field[0]
    wind_y = wind_field[1]
    target = jnp.where(target_mask == 1, -target_depth, target_depth)[:, None, None, :]
    products_x = cosine_row[:, None] * speed_row[None, :]
    products_y = sine_row[:, None] * speed_row[None, :]

    def plane_peak(plane_index):
        row_x = lax.dynamic_slice_in_dim(wind_x, plane_index, 1, 0)
        row_y = lax.dynamic_slice_in_dim(wind_y, plane_index, 1, 0)
        top_x = jnp.max(jnp.abs(products_x[None, :, :, None] + row_x[:, None, None, :]))
        top_y = jnp.max(jnp.abs(products_y[None, :, :, None] + row_y[:, None, None, :]))
        return jnp.stack([top_x, top_y])

    peaks = jnp.max(lax.map(plane_peak, jnp.arange(NX, dtype=jnp.int32)), axis=0)
    peak_x = peaks[0]
    peak_y = peaks[1]
    time_step = courant / (peak_x / spacing + peak_y / spacing + turn_limit / heading_step + thrust_limit / speed_step)
    speeds = speed_row.reshape(1, 1, NV, 1)
    cosines = cosine_row.reshape(1, NTH, 1, 1)
    sines = sine_row.reshape(1, NTH, 1, 1)

    def rate_all(values):
        padded = jnp.pad(values, ((0, 0), (3, 3), (0, 0), (0, 0)), mode="wrap")
        padded = jnp.pad(padded, ((3, 3), (0, 0), (0, 0), (0, 0)), mode="edge")

        def one_block(block_index):
            start = (block_index * 3).astype(jnp.int32)
            block = lax.dynamic_slice_in_dim(padded, start, 9, 0)
            row_x = lax.dynamic_slice_in_dim(wind_x, start, 3, 0)[:, None, None, :]
            row_y = lax.dynamic_slice_in_dim(wind_y, start, 3, 0)[:, None, None, :]
            return hamilton(block, heading_step, speed_step, speeds, cosines, sines, row_x, row_y, peak_x, peak_y)

        blocks = lax.map(one_block, jnp.arange(NX // 3, dtype=jnp.int32))
        return blocks.reshape(NX, NTH, NV, NY)

    section_one = jnp.minimum(level_set + time_step * rate_all(level_set), target)
    section_two = jnp.minimum(0.75 * level_set + 0.25 * (section_one + time_step * rate_all(section_one)), target)
    level_next = jnp.minimum((1.0 / 3.0) * level_set + (2.0 / 3.0) * (section_two + time_step * rate_all(section_two)), target)
    return level_next
```

```python
import functools
import math

import jax
import jax.numpy as jnp
import numpy as np
from jax import lax
from jax.experimental import pallas as pl
from jax.experimental.pallas import tpu as pltpu
from jax.sharding import PartitionSpec as P

MESH = pl.DeviceIdType.MESH
epsilon = 1e-06
courant = 0.5
spacing = 0.05
turn_limit = 1.0
thrust_limit = 0.5
speed_low = 0.5
speed_high = 1.5
NV = 8
NY = 128
NX = 288
NTH = 192
NXL = 9
NHL = 12
HT = 2.0 * math.pi / NTH
HV = (speed_high - speed_low) / (NV - 1)
EPS_X = 0.75 * epsilon * spacing**2
EPS_T = 0.75 * epsilon * HT**2
EPS_V = 0.75 * epsilon * HV**2
K_T = turn_limit * spacing / HT
K_V = thrust_limit * spacing / HV
Z = 16
NEAR = (-3, -2, -1, 1, 2)
FAR = (-5, 5)


def face(p, q, hp, hq, eps, left, mid, right):
    b = q - p
    b2 = b + b
    smooth = (b * b + eps) + hp * q
    out = {"b2": b2}
    if left:
        s = smooth + hq * b2
        out["L"] = 1.0 / (s * s)
        out["aL"] = out["L"] * (1.0 / 3.0)
    if mid:
        out["M"] = 2.0 / (smooth * smooth)
    if right:
        s = smooth - hp * b2
        out["R"] = 1.0 / (s * s)
        out["aR"] = out["R"] * (1.0 / 3.0)
    return out


def join(a_lo, m_lo, c_lo, k_lo, a_hi, m_hi, c_hi, k_hi, c):
    low = (a_lo * k_lo + c_lo * c) / ((a_lo + c_lo) + m_lo)
    high = (a_hi * k_hi + c_hi * c) / ((a_hi + c_hi) + m_hi)
    return high - low, (high + low) - c


def line(load, n, eps):
    u = {i: load(i) for i in range(-3, n + 3)}
    d = {i: u[i + 1] - u[i] for i in range(-3, n + 2)}
    e = {i: d[i] - d[i - 1] for i in range(-2, n + 2)}
    h = {i: 0.75 * e[i] for i in e}
    f = {
        i: face(e[i], e[i + 1], h[i], h[i + 1], eps, i <= n - 2, -1 <= i <= n - 1, i >= 0)
        for i in range(-2, n + 1)
    }
    k = {i: f[i]["b2"] - f[i - 1]["b2"] for i in range(-1, n + 1)}
    g = {i: 6.0 * u[i] - e[i] for i in range(-1, n + 1)}
    result = []
    for i in range(n):
        diff, jump = join(
            f[i - 2]["aL"], f[i - 1]["M"], f[i]["R"], k[i - 1],
            f[i + 1]["aR"], f[i]["M"], f[i - 1]["L"], k[i + 1],
            0.5 * k[i],
        )
        result.append(((g[i + 1] - g[i - 1]) + diff, jump))
    return result


def along(u, axis, eps, first, last):
    n = u.shape[axis]
    back = lambda a: pltpu.roll(a, 1, axis)
    ahead = lambda a: pltpu.roll(a, n - 1, axis)
    d_lo = u - jnp.where(first, u, back(u))
    d_hi = jnp.where(last, u, ahead(u)) - u
    e = d_hi - d_lo
    b_lo = e - jnp.where(first, 0.0, back(e))
    b_hi = jnp.where(last, 0.0, ahead(e)) - e
    p, q = e - b_lo, b_hi + e
    h = 0.75 * e
    m_lo = (b_lo * b_lo + eps) + h * p
    m_hi = (b_hi * b_hi + eps) + h * q
    s_lo = m_lo + h * (b_lo + b_lo)
    s_hi = m_hi - h * (b_hi + b_hi)
    c_hi = 1.0 / (s_lo * s_lo)
    c_lo = 1.0 / (s_hi * s_hi)
    c = b_hi - b_lo
    k = c + c
    e2 = e + e
    flat = 1.0 / (3.0 * eps * eps)
    a_lo = jnp.where(first, flat, back(c_hi * (1.0 / 3.0)))
    a_hi = jnp.where(last, flat, ahead(c_lo * (1.0 / 3.0)))
    k_lo = jnp.where(first, e2, back(k))
    k_hi = jnp.where(last, e2, ahead(k))
    diff, jump = join(a_lo, 2.0 / (m_lo * m_lo), c_lo, k_lo, a_hi, 2.0 / (m_hi * m_hi), c_hi, k_hi, c)
    return (6.0 * (d_hi + d_lo) - (b_hi + b_lo)) + diff, jump


def iotas():
    shape = (NV, NY)
    row = lax.broadcasted_iota(jnp.int32, shape, 0)
    lane = lax.broadcasted_iota(jnp.int32, shape, 1)
    return row, lane


def speeds_of(row):
    return speed_low + row.astype(jnp.float32) * np.float32(HV)


def pass_vy(u_ref, r_ref, wy_ref, tab_ref, by_ref, pk_ref, lo, hi):
    def body(x, carry):
        row, lane = iotas()
        speeds = speeds_of(row)
        v0, v1 = row == 0, row == NV - 1
        y0, y1 = lane == 0, lane == NY - 1
        wind = wy_ref[x]
        for h in range(NHL):
            u = u_ref[x + 3, h + 3]
            total_v, jump_v = along(u, 0, EPS_V, v0, v1)
            total_y, jump_y = along(u, 1, EPS_X, y0, y1)
            flow = speeds * tab_ref[NHL + h : NHL + h + 1, :] + wind
            rate = total_y * flow + K_V * (jump_v - jnp.abs(total_v))
            if by_ref is not None:
                by_ref[x, h] = jump_y
            else:
                rate = rate + pk_ref[1] * jump_y
            r_ref[x, h] = rate
        return carry

    lax.fori_loop(lo, hi, body, 0)


def pass_h(u_ref, r_ref, lo, hi):
    def body(x, carry):
        for h, (total, jump) in enumerate(line(lambda i: u_ref[x + 3, i + 3], NHL, EPS_T)):
            r_ref[x, h] = r_ref[x, h] + K_T * (jump - jnp.abs(total))
        return carry

    lax.fori_loop(lo, hi, body, 0)


def pass_x(u_ref, wx_ref, tab_ref, lo, finish, group=4):
    def body(t, carry):
        row, _ = iotas()
        speeds = speeds_of(row)
        for j in range(group):
            h = t * group + j
            lanes = speeds * tab_ref[pl.ds(h, 1), :]
            cells = line(lambda i: u_ref[lo + i + 3, h + 3], 3, EPS_X)
            for i, (total, jump) in enumerate(cells):
                finish(lo + i, h, total * (lanes + wx_ref[lo + i]), jump)
        return carry

    lax.fori_loop(0, NHL // group, body, 0)


def bounds():
    speeds = np.float32(speed_low) + np.arange(NV, dtype=np.float32) * np.float32(HV)
    angles = np.arange(NTH, dtype=np.float32) * np.float32(HT)
    px = np.cos(angles)[:, None] * speeds
    py = np.sin(angles)[:, None] * speeds
    return [float(a) for a in (px.max(), -px.min(), py.max(), -py.min())]


def table():
    angles = np.arange(NTH, dtype=np.float32) * np.float32(HT)
    both = np.stack([np.cos(angles).reshape(-1, NHL), np.sin(angles).reshape(-1, NHL)], 1)
    both = both.reshape(NTH // NHL, 2 * NHL, 1).astype(np.float32)
    return np.broadcast_to(both, (NTH // NHL, 2 * NHL, NY)).copy()


def kernel(
    level, wind, mask, depth, tab_all, out,
    u0, u1, u2, r, bx, by, res, wv, mv, dv, tab, wx, wy, tg, pk, pbuf, pmine,
    sem_in, sx, rx, sh, rh, sp, rp, so,
):
    g = lax.axis_index("gx")
    hd = lax.axis_index("head")
    ng, nh = lax.axis_size("gx"), lax.axis_size("head")
    yh, z = g // Z, g % Z
    ring = lambda o: yh * Z + (z + Z + o) % Z
    fields = (u0, u1, u2)

    barrier = pltpu.get_barrier_semaphore()
    peers = [
        {"gx": (g + 1) % ng, "head": hd},
        {"gx": (g + ng - 1) % ng, "head": hd},
        {"gx": g, "head": (hd + 1) % nh},
        {"gx": g, "head": (hd + nh - 1) % nh},
        {"gx": (g + Z) % ng, "head": (hd + nh // 2) % nh},
    ] + [{"gx": ring(o), "head": hd} for o in (-3, -2, -1, 1, 2, 3)]
    for peer in peers:
        pl.semaphore_signal(barrier, inc=1, device_id=peer, device_id_type=MESH)

    get_wind = pltpu.make_async_copy(wind, wv, sem_in.at[0])
    get_wind.start()
    get_level = pltpu.make_async_copy(level, u0.at[pl.ds(3, NXL), pl.ds(3, NHL)], sem_in.at[1])
    get_level.start()
    get_tab = pltpu.make_async_copy(tab_all.at[hd], tab, sem_in.at[2])
    get_tab.start()
    get_mask = pltpu.make_async_copy(mask, mv, sem_in.at[3])
    get_mask.start()
    get_depth = pltpu.make_async_copy(depth, dv, sem_in.at[4])
    get_depth.start()

    get_wind.wait()
    for i in range(NXL):
        wx[i] = jnp.broadcast_to(wv[0, i : i + 1, :], (NV, NY))
        wy[i] = jnp.broadcast_to(wv[1, i : i + 1, :], (NV, NY))
    tops = []
    for c in range(2):
        top, low = wv[c, 0:1, :], wv[c, 0:1, :]
        for i in range(1, NXL):
            top, low = jnp.maximum(top, wv[c, i : i + 1, :]), jnp.minimum(low, wv[c, i : i + 1, :])
        tops += [top, -low]
    row, _ = iotas()
    tile = jnp.broadcast_to(tops[0], (NV, NY))
    for i in range(1, 4):
        tile = jnp.where(row == i, jnp.broadcast_to(tops[i], (NV, NY)), tile)
    for shift in (1, 2, 4, 8, 16, 32, 64):
        tile = jnp.maximum(tile, pltpu.roll(tile, shift, 1))
    pmine[0] = tile

    def x_copy(s, up):
        src = level if s == 0 else fields[s]
        base = 0 if s == 0 else 3
        start = (NXL - 3 if up else 0) + base
        return pltpu.make_async_remote_copy(
            src_ref=src.at[pl.ds(start, 3), pl.ds(base, NHL)],
            dst_ref=fields[s].at[pl.ds(0 if up else NXL + 3, 3), pl.ds(3, NHL)],
            send_sem=sx.at[s, int(up)],
            recv_sem=rx.at[s, int(up)],
            device_id={"gx": (g + 1) % ng if up else (g + ng - 1) % ng, "head": hd},
            device_id_type=MESH,
        )

    def h_copy(s, up, chunk):
        src = level if s == 0 else fields[s]
        base = 0 if s == 0 else 3
        start = (NHL - 3 if up else 0) + base
        return pltpu.make_async_remote_copy(
            src_ref=src.at[pl.ds(3 * chunk + base, 3), pl.ds(start, 3)],
            dst_ref=fields[s].at[pl.ds(3 * chunk + 3, 3), pl.ds(0 if up else NHL + 3, 3)],
            send_sem=sh.at[s, int(up), chunk],
            recv_sem=rh.at[s, int(up), chunk],
            device_id={"gx": g, "head": (hd + 1) % nh if up else (hd + nh - 1) % nh},
            device_id_type=MESH,
        )

    def send_x(s, up):
        @pl.when(g < ng - 1 if up else g > 0)
        def _():
            x_copy(s, up).start()

    def take_x(s, up):
        @pl.when(g > 0 if up else g < ng - 1)
        def _():
            x_copy(s, up).wait_recv()

        @pl.when(g == 0 if up else g == ng - 1)
        def _():
            for h in range(NHL):
                edge = fields[s][3 if up else NXL + 2, h + 3]
                for i in range(3):
                    fields[s][i if up else NXL + 3 + i, h + 3] = edge

    def send_h(s, chunk):
        for up in (True, False):
            h_copy(s, up, chunk).start()

    def take_h(s, chunk):
        for up in (True, False):
            h_copy(s, up, chunk).wait_recv()

    def p_copy(slot, src, dst, to):
        return pltpu.make_async_remote_copy(
            src_ref=pmine.at[src], dst_ref=pbuf.at[dst], send_sem=sp.at[slot], recv_sem=rp.at[slot],
            device_id=to, device_id_type=MESH,
        )

    p_first = [p_copy(0, 0, 0, peers[4])]
    p_near = [p_copy(1 + j, 1, 1 + j, {"gx": ring(o), "head": hd}) for j, o in enumerate(NEAR)]
    p_far = [p_copy(6 + j, 2, 6 + j, {"gx": ring(o), "head": hd}) for j, o in enumerate(FAR)]

    def fold(copies, src, dst):
        best = pmine[src]
        for c in copies:
            c.wait_recv()
        first = {1: 0, 2: 1, 3: 6}[dst]
        for j in range(len(copies)):
            best = jnp.maximum(best, pbuf[first + j])
        pmine[dst] = best

    pl.semaphore_wait(barrier, len(peers))
    for c in p_first:
        c.start()
    send_x(0, True)
    send_x(0, False)
    for chunk in range(3):
        send_h(0, chunk)

    get_mask.wait()
    get_depth.wait()
    for i in range(NXL):
        d = dv[i : i + 1, :]
        tg[i] = jnp.broadcast_to(jnp.where(mv[i : i + 1, :] == 1, -d, d), (NV, NY))
    get_tab.wait()
    get_level.wait()

    pass_vy(u0, r, wy, tab, by, None, 0, 3)
    fold(p_first, 0, 1)
    for c in p_near:
        c.start()
    pass_vy(u0, r, wy, tab, by, None, 3, NXL)
    for chunk in range(3):
        take_h(0, chunk)
    pass_h(u0, r, 0, NXL)
    fold(p_near, 1, 2)
    for c in p_far:
        c.start()

    def keep(x, h, part, jump):
        r[x, h] = r[x, h] + part
        bx[x, h] = jump

    pass_x(u0, wx, tab, 3, keep)
    take_x(0, True)
    pass_x(u0, wx, tab, 0, keep)
    take_x(0, False)
    pass_x(u0, wx, tab, 6, keep)

    fold(p_far, 2, 3)
    top = pmine[3]
    cx, cnx, cy, cny = bounds()
    peak_x = jnp.maximum(top[0:1] + cx, top[1:2] + cnx)
    peak_y = jnp.maximum(top[2:3] + cy, top[3:4] + cny)
    step = courant / (peak_x / spacing + peak_y / spacing + turn_limit / HT + thrust_limit / HV)
    pk[0] = jnp.broadcast_to(peak_x, (NV, NY))
    pk[1] = jnp.broadcast_to(peak_y, (NV, NY))
    pk[2] = jnp.broadcast_to(step * (1.0 / (12.0 * spacing)), (NV, NY))

    def update_one(lo):
        def body(h, carry):
            px, py, dt = pk[0], pk[1], pk[2]
            for i in range(3):
                rate = r[lo + i, h] + px * bx[lo + i, h] + py * by[lo + i, h]
                u1[lo + i + 3, h + 3] = jnp.minimum(u0[lo + i + 3, h + 3] + dt * rate, tg[lo + i])
            return carry

        lax.fori_loop(0, NHL, body, 0, unroll=2)

    update_one(0)
    send_x(1, False)
    send_h(1, 0)
    update_one(6)
    send_x(1, True)
    send_h(1, 2)
    update_one(3)
    send_h(1, 1)

    def section(s, write, after):
        u = fields[s]
        old, new = (0.75, 0.25) if s == 1 else (1.0 / 3.0, 2.0 / 3.0)
        pass_vy(u, r, wy, tab, None, pk, 0, NXL)
        for chunk in (0, 2, 1):
            take_h(s, chunk)
            pass_h(u, r, 3 * chunk, 3 * chunk + 3)

        def finish(x, h, part, jump):
            rate = (r[x, h] + part) + pk[0] * jump
            now = old * u0[x + 3, h + 3] + new * (u[x + 3, h + 3] + pk[2] * rate)
            write(x, h, jnp.minimum(now, tg[x]))

        pass_x(u, wx, tab, 3, finish)
        after(1)
        take_x(s, True)
        pass_x(u, wx, tab, 0, finish)
        after(0)
        take_x(s, False)
        pass_x(u, wx, tab, 6, finish)
        after(2)

    def write_two(x, h, value):
        u2[x + 3, h + 3] = value

    def after_two(chunk):
        if chunk != 1:
            send_x(2, chunk == 2)
        send_h(2, chunk)

    section(1, write_two, after_two)

    def write_out(x, h, value):
        res[x, h] = value

    puts = [
        pltpu.make_async_copy(res.at[pl.ds(3 * c, 3)], out.at[pl.ds(3 * c, 3)], so.at[c]) for c in range(3)
    ]
    section(2, write_out, lambda chunk: puts[chunk].start())

    for put in puts:
        put.wait()
    for c in p_first + p_near + p_far:
        c.wait_send()
    for s in range(3):
        for up in (True, False):

            @pl.when(g < ng - 1 if up else g > 0)
            def _():
                x_copy(s, up).wait_send()

            for chunk in range(3):
                h_copy(s, up, chunk).wait_send()


def local(level_set, wind_field, target_mask, target_depth):
    field = pltpu.VMEM((NXL + 6, NHL + 6, NV, NY), jnp.float32)
    inner = pltpu.VMEM((NXL, NHL, NV, NY), jnp.float32)
    rows = pltpu.VMEM((NXL, NV, NY), jnp.float32)
    dma = pltpu.SemaphoreType.DMA
    return pl.pallas_call(
        kernel,
        out_shape=jax.ShapeDtypeStruct(level_set.shape, jnp.float32),
        in_specs=[pl.BlockSpec(memory_space=pl.ANY)] * 5,
        out_specs=pl.BlockSpec(memory_space=pl.ANY),
        scratch_shapes=[
            field, field, field, inner, inner, inner, inner,
            pltpu.VMEM((2, NXL, NY), jnp.float32),
            pltpu.VMEM((NXL, NY), jnp.int32),
            pltpu.VMEM((NXL, NY), jnp.float32),
            pltpu.VMEM((2 * NHL, NY), jnp.float32),
            rows, rows, rows,
            pltpu.VMEM((3, NV, NY), jnp.float32),
            pltpu.VMEM((8, NV, NY), jnp.float32),
            pltpu.VMEM((4, NV, NY), jnp.float32),
            dma((5,)), dma((3, 2)), dma((3, 2)), dma((3, 2, 3)), dma((3, 2, 3)), dma((8,)), dma((8,)), dma((3,)),
        ],
        compiler_params=pltpu.CompilerParams(collective_id=0, has_side_effects=True),
        name="step",
    )(level_set, wind_field, target_mask, target_depth, jnp.asarray(table()))


def solution(mesh):
    return jax.shard_map(
        local,
        mesh=mesh,
        in_specs=(P("gx", "head", None, None), P(None, "gx", None), P("gx", None), P("gx", None)),
        out_specs=P("gx", "head", None, None),
        check_vma=False,
    )
```

```python
import functools
import math

import jax
import jax.numpy as jnp
import numpy as np
from jax import lax
from jax.experimental import pallas as pl
from jax.experimental.pallas import tpu as pltpu
from jax.sharding import PartitionSpec as P

MESH = pl.DeviceIdType.MESH
epsilon = 1e-06
courant = 0.5
spacing = 0.05
turn_limit = 1.0
thrust_limit = 0.5
speed_low = 0.5
speed_high = 1.5
NV = 8
NY = 128
NX = 288
NTH = 192
NXL = 9
NHL = 12
HT = 2.0 * math.pi / NTH
HV = (speed_high - speed_low) / (NV - 1)
EPS_X = 0.75 * epsilon * spacing**2
EPS_T = 0.75 * epsilon * HT**2
EPS_V = 0.75 * epsilon * HV**2
K_T = turn_limit * spacing / HT
K_V = thrust_limit * spacing / HV
Z = 16


def face(p, q, hp, hq, eps, left, mid, right):
    b = q - p
    b2 = b + b
    smooth = (b * b + eps) + hp * q
    out = {"b2": b2}
    if left:
        s = smooth + hq * b2
        out["L"] = 1.0 / (s * s)
        out["aL"] = out["L"] * (1.0 / 3.0)
    if mid:
        out["M"] = 2.0 / (smooth * smooth)
    if right:
        s = smooth - hp * b2
        out["R"] = 1.0 / (s * s)
        out["aR"] = out["R"] * (1.0 / 3.0)
    return out


def join(a_lo, m_lo, c_lo, k_lo, a_hi, m_hi, c_hi, k_hi, c):
    low = (a_lo * k_lo + c_lo * c) / ((a_lo + c_lo) + m_lo)
    high = (a_hi * k_hi + c_hi * c) / ((a_hi + c_hi) + m_hi)
    return high - low, (high + low) - c


def line(load, n, eps):
    u = {i: load(i) for i in range(-3, n + 3)}
    d = {i: u[i + 1] - u[i] for i in range(-3, n + 2)}
    e = {i: d[i] - d[i - 1] for i in range(-2, n + 2)}
    h = {i: 0.75 * e[i] for i in e}
    f = {
        i: face(e[i], e[i + 1], h[i], h[i + 1], eps, i <= n - 2, -1 <= i <= n - 1, i >= 0)
        for i in range(-2, n + 1)
    }
    k = {i: f[i]["b2"] - f[i - 1]["b2"] for i in range(-1, n + 1)}
    g = {i: 6.0 * u[i] - e[i] for i in range(-1, n + 1)}
    result = []
    for i in range(n):
        diff, jump = join(
            f[i - 2]["aL"], f[i - 1]["M"], f[i]["R"], k[i - 1],
            f[i + 1]["aR"], f[i]["M"], f[i - 1]["L"], k[i + 1],
            0.5 * k[i],
        )
        result.append(((g[i + 1] - g[i - 1]) + diff, jump))
    return result


def along(u, axis, eps, first, last):
    n = u.shape[axis]
    back = lambda a: pltpu.roll(a, 1, axis)
    ahead = lambda a: pltpu.roll(a, n - 1, axis)
    d_lo = u - jnp.where(first, u, back(u))
    d_hi = jnp.where(last, u, ahead(u)) - u
    e = d_hi - d_lo
    b_lo = e - jnp.where(first, 0.0, back(e))
    b_hi = jnp.where(last, 0.0, ahead(e)) - e
    p, q = e - b_lo, b_hi + e
    h = 0.75 * e
    m_lo = (b_lo * b_lo + eps) + h * p
    m_hi = (b_hi * b_hi + eps) + h * q
    s_lo = m_lo + h * (b_lo + b_lo)
    s_hi = m_hi - h * (b_hi + b_hi)
    c_hi = 1.0 / (s_lo * s_lo)
    c_lo = 1.0 / (s_hi * s_hi)
    c = b_hi - b_lo
    k = c + c
    e2 = e + e
    flat = 1.0 / (3.0 * eps * eps)
    a_lo = jnp.where(first, flat, back(c_hi * (1.0 / 3.0)))
    a_hi = jnp.where(last, flat, ahead(c_lo * (1.0 / 3.0)))
    k_lo = jnp.where(first, e2, back(k))
    k_hi = jnp.where(last, e2, ahead(k))
    diff, jump = join(a_lo, 2.0 / (m_lo * m_lo), c_lo, k_lo, a_hi, 2.0 / (m_hi * m_hi), c_hi, k_hi, c)
    return (6.0 * (d_hi + d_lo) - (b_hi + b_lo)) + diff, jump


def iotas():
    shape = (NV, NY)
    row = lax.broadcasted_iota(jnp.int32, shape, 0)
    lane = lax.broadcasted_iota(jnp.int32, shape, 1)
    return row, lane


def speeds_of(row):
    return speed_low + row.astype(jnp.float32) * np.float32(HV)


def pass_vy(u_ref, r_ref, wy_ref, tab_ref, by_ref, pk_ref, lo, hi):
    def body(x, carry):
        row, lane = iotas()
        speeds = speeds_of(row)
        v0, v1 = row == 0, row == NV - 1
        y0, y1 = lane == 0, lane == NY - 1
        wind = wy_ref[x]
        for h in range(NHL):
            u = u_ref[x + 3, h + 3]
            total_v, jump_v = along(u, 0, EPS_V, v0, v1)
            total_y, jump_y = along(u, 1, EPS_X, y0, y1)
            flow = speeds * tab_ref[NHL + h : NHL + h + 1, :] + wind
            rate = total_y * flow + K_V * (jump_v - jnp.abs(total_v))
            if by_ref is not None:
                by_ref[x, h] = jump_y
            else:
                rate = rate + pk_ref[1] * jump_y
            r_ref[x, h] = rate
        return carry

    lax.fori_loop(lo, hi, body, 0)


def pass_h(u_ref, r_ref, lo, hi):
    def body(x, carry):
        for h, (total, jump) in enumerate(line(lambda i: u_ref[x + 3, i + 3], NHL, EPS_T)):
            r_ref[x, h] = r_ref[x, h] + K_T * (jump - jnp.abs(total))
        return carry

    lax.fori_loop(lo, hi, body, 0)


def pass_x(u_ref, wx_ref, tab_ref, lo, finish, group=4):
    def body(t, carry):
        row, _ = iotas()
        speeds = speeds_of(row)
        for j in range(group):
            h = t * group + j
            lanes = speeds * tab_ref[pl.ds(h, 1), :]
            cells = line(lambda i: u_ref[lo + i + 3, h + 3], 3, EPS_X)
            for i, (total, jump) in enumerate(cells):
                finish(lo + i, h, total * (lanes + wx_ref[lo + i]), jump)
        return carry

    lax.fori_loop(0, NHL // group, body, 0)


def bounds():
    speeds = np.float32(speed_low) + np.arange(NV, dtype=np.float32) * np.float32(HV)
    angles = np.arange(NTH, dtype=np.float32) * np.float32(HT)
    px = np.cos(angles)[:, None] * speeds
    py = np.sin(angles)[:, None] * speeds
    return [float(a) for a in (px.max(), -px.min(), py.max(), -py.min())]


def table():
    angles = np.arange(NTH, dtype=np.float32) * np.float32(HT)
    both = np.stack([np.cos(angles).reshape(-1, NHL), np.sin(angles).reshape(-1, NHL)], 1)
    both = both.reshape(NTH // NHL, 2 * NHL, 1).astype(np.float32)
    return np.broadcast_to(both, (NTH // NHL, 2 * NHL, NY)).copy()


def kernel(
    level, wind, mask, depth, tab_all, out,
    u0, u1, u2, r, bx, by, res, wv, mv, dv, tab, wx, wy, tg, pk, pbuf, pmine,
    sem_in, sx, rx, sh, rh, sp, rp, so,
):
    g = lax.axis_index("gx")
    hd = lax.axis_index("head")
    ng, nh = lax.axis_size("gx"), lax.axis_size("head")
    yh, z = g // Z, g % Z
    at = lambda half, z_: half * Z + z_
    across = (hd + nh // 2) % nh
    fields = (u0, u1, u2)

    barrier = pltpu.get_barrier_semaphore()

    def greet(peer):
        pl.semaphore_signal(barrier, inc=1, device_id=peer, device_id_type=MESH)

    greet({"gx": g, "head": (hd + 1) % nh})
    greet({"gx": g, "head": (hd + nh - 1) % nh})

    @pl.when(g < ng - 1)
    def _():
        greet({"gx": (g + 1) % ng, "head": hd})

    @pl.when(g > 0)
    def _():
        greet({"gx": (g + ng - 1) % ng, "head": hd})

    @pl.when(z == 0)
    def _():
        for i in range(1, Z):
            greet({"gx": at(yh, i), "head": hd})
        for i in range(Z):
            greet({"gx": at(1 - yh, i), "head": across})

    get_wind = pltpu.make_async_copy(wind, wv, sem_in.at[0])
    get_wind.start()
    get_level = pltpu.make_async_copy(level, u0.at[pl.ds(3, NXL), pl.ds(3, NHL)], sem_in.at[1])
    get_level.start()
    get_tab = pltpu.make_async_copy(tab_all.at[hd], tab, sem_in.at[2])
    get_tab.start()
    get_mask = pltpu.make_async_copy(mask, mv, sem_in.at[3])
    get_mask.start()
    get_depth = pltpu.make_async_copy(depth, dv, sem_in.at[4])
    get_depth.start()

    get_wind.wait()
    tops = []
    for c in range(2):
        top, low = wv[0, c : c + 1, :], wv[0, c : c + 1, :]
        for i in range(1, NXL):
            top, low = jnp.maximum(top, wv[i, c : c + 1, :]), jnp.minimum(low, wv[i, c : c + 1, :])
        tops += [top, -low]
    row, _ = iotas()
    tile = jnp.broadcast_to(tops[0], (NV, NY))
    for i in range(1, 4):
        tile = jnp.where(row == i, jnp.broadcast_to(tops[i], (NV, NY)), tile)
    pmine[0] = jnp.broadcast_to(jnp.max(tile, axis=1, keepdims=True), (NV, NY))

    def x_copy(s, up):
        src = level if s == 0 else fields[s]
        base = 0 if s == 0 else 3
        start = (NXL - 3 if up else 0) + base
        return pltpu.make_async_remote_copy(
            src_ref=src.at[pl.ds(start, 3), pl.ds(base, NHL)],
            dst_ref=fields[s].at[pl.ds(0 if up else NXL + 3, 3), pl.ds(3, NHL)],
            send_sem=sx.at[s, int(up)],
            recv_sem=rx.at[s, int(up)],
            device_id={"gx": (g + 1) % ng if up else (g + ng - 1) % ng, "head": hd},
            device_id_type=MESH,
        )

    def h_copy(s, up, chunk):
        src = level if s == 0 else fields[s]
        base = 0 if s == 0 else 3
        start = (NHL - 3 if up else 0) + base
        return pltpu.make_async_remote_copy(
            src_ref=src.at[pl.ds(3 * chunk + base, 3), pl.ds(start, 3)],
            dst_ref=fields[s].at[pl.ds(3 * chunk + 3, 3), pl.ds(0 if up else NHL + 3, 3)],
            send_sem=sh.at[s, int(up), chunk],
            recv_sem=rh.at[s, int(up), chunk],
            device_id={"gx": g, "head": (hd + 1) % nh if up else (hd + nh - 1) % nh},
            device_id_type=MESH,
        )

    def send_x(s, up):
        @pl.when(g < ng - 1 if up else g > 0)
        def _():
            x_copy(s, up).start()

    def take_x(s, up):
        @pl.when(g > 0 if up else g < ng - 1)
        def _():
            x_copy(s, up).wait_recv()

        @pl.when(g == 0 if up else g == ng - 1)
        def _():
            for h in range(NHL):
                edge = fields[s][3 if up else NXL + 2, h + 3]
                for i in range(3):
                    fields[s][i if up else NXL + 3 + i, h + 3] = edge

    def send_h(s, chunk):
        for up in (True, False):
            h_copy(s, up, chunk).start()

    def take_h(s, chunk):
        for up in (True, False):
            h_copy(s, up, chunk).wait_recv()

    to_root = lambda: pltpu.make_async_remote_copy(
        src_ref=pmine.at[0], dst_ref=pbuf.at[z], send_sem=sp.at[0], recv_sem=rp.at[z],
        device_id={"gx": at(yh, 0), "head": hd}, device_id_type=MESH,
    )
    to_other = lambda: pltpu.make_async_remote_copy(
        src_ref=pmine.at[0], dst_ref=pbuf.at[Z + z], send_sem=sp.at[1], recv_sem=rp.at[Z + z],
        device_id={"gx": at(1 - yh, 0), "head": across}, device_id_type=MESH,
    )
    answer = lambda i: pltpu.make_async_remote_copy(
        src_ref=pmine.at[1], dst_ref=pbuf.at[2 * Z], send_sem=sp.at[1 + i], recv_sem=rp.at[2 * Z],
        device_id={"gx": at(yh, i), "head": hd}, device_id_type=MESH,
    )
    arrived = lambda slot: pltpu.make_async_remote_copy(
        src_ref=pmine.at[0], dst_ref=pbuf.at[slot], send_sem=sp.at[0], recv_sem=rp.at[slot],
        device_id={"gx": at(1 - yh, 0), "head": across}, device_id_type=MESH,
    )

    greeters = 3 + (g > 0).astype(jnp.int32) + (g < ng - 1).astype(jnp.int32) + (z > 0).astype(jnp.int32)
    pl.semaphore_wait(barrier, greeters)

    @pl.when(z > 0)
    def _():
        to_root().start()

    to_other().start()
    send_x(0, True)
    send_x(0, False)
    for chunk in range(3):
        send_h(0, chunk)

    for i in range(NXL):
        wx[i] = jnp.broadcast_to(wv[i, 0:1, :], (NV, NY))
        wy[i] = jnp.broadcast_to(wv[i, 1:2, :], (NV, NY))
    get_mask.wait()
    get_depth.wait()
    for i in range(NXL):
        d = dv[i : i + 1, :]
        tg[i] = jnp.broadcast_to(jnp.where(mv[i : i + 1, :] == 1, -d, d), (NV, NY))
    get_tab.wait()
    get_level.wait()

    pass_vy(u0, r, wy, tab, by, None, 0, NXL)
    for chunk in range(3):
        take_h(0, chunk)
    pass_h(u0, r, 0, NXL)

    def keep(x, h, part, jump):
        r[x, h] = r[x, h] + part
        bx[x, h] = jump

    pass_x(u0, wx, tab, 3, keep)
    take_x(0, True)
    pass_x(u0, wx, tab, 0, keep)
    take_x(0, False)
    pass_x(u0, wx, tab, 6, keep)

    @pl.when(z == 0)
    def _():
        best = pmine[0]
        for slot in range(1, 2 * Z):
            arrived(slot).wait_recv()
            best = jnp.maximum(best, pbuf[slot])
        pmine[1] = best
        for i in range(1, Z):
            answer(i).start()

    @pl.when(z > 0)
    def _():
        arrived(2 * Z).wait_recv()
        pmine[1] = pbuf[2 * Z]

    top = pmine[1]
    cx, cnx, cy, cny = bounds()
    peak_x = jnp.maximum(top[0:1] + cx, top[1:2] + cnx)
    peak_y = jnp.maximum(top[2:3] + cy, top[3:4] + cny)
    step = courant / (peak_x / spacing + peak_y / spacing + turn_limit / HT + thrust_limit / HV)
    pk[0] = jnp.broadcast_to(peak_x, (NV, NY))
    pk[1] = jnp.broadcast_to(peak_y, (NV, NY))
    pk[2] = jnp.broadcast_to(step * (1.0 / (12.0 * spacing)), (NV, NY))

    def update_one(lo):
        def body(h, carry):
            px, py, dt = pk[0], pk[1], pk[2]
            for i in range(3):
                rate = r[lo + i, h] + px * bx[lo + i, h] + py * by[lo + i, h]
                u1[lo + i + 3, h + 3] = jnp.minimum(u0[lo + i + 3, h + 3] + dt * rate, tg[lo + i])
            return carry

        lax.fori_loop(0, NHL, body, 0, unroll=2)

    update_one(0)
    send_x(1, False)
    send_h(1, 0)
    update_one(6)
    send_x(1, True)
    send_h(1, 2)
    update_one(3)
    send_h(1, 1)

    def section(s, write, after):
        u = fields[s]
        old, new = (0.75, 0.25) if s == 1 else (1.0 / 3.0, 2.0 / 3.0)
        pass_vy(u, r, wy, tab, None, pk, 0, NXL)
        for chunk in (0, 2, 1):
            take_h(s, chunk)
            pass_h(u, r, 3 * chunk, 3 * chunk + 3)

        def finish(x, h, part, jump):
            rate = (r[x, h] + part) + pk[0] * jump
            now = old * u0[x + 3, h + 3] + new * (u[x + 3, h + 3] + pk[2] * rate)
            write(x, h, jnp.minimum(now, tg[x]))

        pass_x(u, wx, tab, 3, finish)
        after(1)
        take_x(s, True)
        pass_x(u, wx, tab, 0, finish)
        after(0)
        take_x(s, False)
        pass_x(u, wx, tab, 6, finish)
        after(2)

    def write_two(x, h, value):
        u2[x + 3, h + 3] = value

    def after_two(chunk):
        if chunk != 1:
            send_x(2, chunk == 2)
        send_h(2, chunk)

    section(1, write_two, after_two)

    def write_out(x, h, value):
        res[x, h] = value

    puts = [
        pltpu.make_async_copy(res.at[pl.ds(3 * c, 3)], out.at[pl.ds(3 * c, 3)], so.at[c]) for c in range(3)
    ]
    section(2, write_out, lambda chunk: puts[chunk].start())

    for put in puts:
        put.wait()

    @pl.when(z > 0)
    def _():
        to_root().wait_send()

    to_other().wait_send()

    @pl.when(z == 0)
    def _():
        for i in range(1, Z):
            answer(i).wait_send()

    for s in range(3):
        for up in (True, False):

            @pl.when(g < ng - 1 if up else g > 0)
            def _():
                x_copy(s, up).wait_send()

            for chunk in range(3):
                h_copy(s, up, chunk).wait_send()


def local(level_set, wind_field, target_mask, target_depth):
    field = pltpu.VMEM((NXL + 6, NHL + 6, NV, NY), jnp.float32)
    inner = pltpu.VMEM((NXL, NHL, NV, NY), jnp.float32)
    rows = pltpu.VMEM((NXL, NV, NY), jnp.float32)
    dma = pltpu.SemaphoreType.DMA
    return pl.pallas_call(
        kernel,
        out_shape=jax.ShapeDtypeStruct(level_set.shape, jnp.float32),
        in_specs=[pl.BlockSpec(memory_space=pl.ANY)] * 5,
        out_specs=pl.BlockSpec(memory_space=pl.ANY),
        scratch_shapes=[
            field, field, field, inner, inner, inner, inner,
            pltpu.VMEM((NXL, 2, NY), jnp.float32),
            pltpu.VMEM((NXL, NY), jnp.int32),
            pltpu.VMEM((NXL, NY), jnp.float32),
            pltpu.VMEM((2 * NHL, NY), jnp.float32),
            rows, rows, rows,
            pltpu.VMEM((3, NV, NY), jnp.float32),
            pltpu.VMEM((2 * Z + 1, NV, NY), jnp.float32),
            pltpu.VMEM((2, NV, NY), jnp.float32),
            dma((5,)), dma((3, 2)), dma((3, 2)), dma((3, 2, 3)), dma((3, 2, 3)), dma((Z + 1,)), dma((2 * Z + 1,)), dma((3,)),
        ],
        compiler_params=pltpu.CompilerParams(collective_id=0, has_side_effects=True),
        name="step",
    )(level_set, jnp.transpose(wind_field, (1, 0, 2)), target_mask, target_depth, jnp.asarray(table()))


def solution(mesh):
    return jax.shard_map(
        local,
        mesh=mesh,
        in_specs=(P("gx", "head", None, None), P(None, "gx", None), P("gx", None), P("gx", None)),
        out_specs=P("gx", "head", None, None),
        check_vma=False,
    )
```

```python
import functools
import math

import jax
import jax.numpy as jnp
import numpy as np
from jax import lax
from jax.experimental import pallas as pl
from jax.experimental.pallas import tpu as pltpu
from jax.sharding import PartitionSpec as P

MESH = pl.DeviceIdType.MESH
epsilon = 1e-06
courant = 0.5
spacing = 0.05
turn_limit = 1.0
thrust_limit = 0.5
speed_low = 0.5
speed_high = 1.5
NV = 8
NY = 128
NX = 288
NTH = 192
NXL = 9
NHL = 12
HT = 2.0 * math.pi / NTH
HV = (speed_high - speed_low) / (NV - 1)
EPS_X = 0.75 * epsilon * spacing**2
EPS_T = 0.75 * epsilon * HT**2
EPS_V = 0.75 * epsilon * HV**2
K_T = turn_limit * spacing / HT
K_V = thrust_limit * spacing / HV
Z = 16


def face(p, q, hp, hq, eps, left, mid, right):
    b = q - p
    b2 = b + b
    smooth = (b * b + eps) + hp * q
    out = {"b2": b2}
    if left:
        s = smooth + hq * b2
        out["L"] = 1.0 / (s * s)
        out["aL"] = out["L"] * (1.0 / 3.0)
    if mid:
        out["M"] = 2.0 / (smooth * smooth)
    if right:
        s = smooth - hp * b2
        out["R"] = 1.0 / (s * s)
        out["aR"] = out["R"] * (1.0 / 3.0)
    return out


def join(a_lo, m_lo, c_lo, k_lo, a_hi, m_hi, c_hi, k_hi, c):
    low = (a_lo * k_lo + c_lo * c) / ((a_lo + c_lo) + m_lo)
    high = (a_hi * k_hi + c_hi * c) / ((a_hi + c_hi) + m_hi)
    return high - low, (high + low) - c


def line(load, n, eps):
    u = {i: load(i) for i in range(-3, n + 3)}
    d = {i: u[i + 1] - u[i] for i in range(-3, n + 2)}
    e = {i: d[i] - d[i - 1] for i in range(-2, n + 2)}
    h = {i: 0.75 * e[i] for i in e}
    f = {
        i: face(e[i], e[i + 1], h[i], h[i + 1], eps, i <= n - 2, -1 <= i <= n - 1, i >= 0)
        for i in range(-2, n + 1)
    }
    k = {i: f[i]["b2"] - f[i - 1]["b2"] for i in range(-1, n + 1)}
    g = {i: 6.0 * u[i] - e[i] for i in range(-1, n + 1)}
    result = []
    for i in range(n):
        diff, jump = join(
            f[i - 2]["aL"], f[i - 1]["M"], f[i]["R"], k[i - 1],
            f[i + 1]["aR"], f[i]["M"], f[i - 1]["L"], k[i + 1],
            0.5 * k[i],
        )
        result.append(((g[i + 1] - g[i - 1]) + diff, jump))
    return result


def along(u, axis, eps, first, last):
    n = u.shape[axis]
    back = lambda a: pltpu.roll(a, 1, axis)
    ahead = lambda a: pltpu.roll(a, n - 1, axis)
    d_lo = u - jnp.where(first, u, back(u))
    d_hi = jnp.where(last, u, ahead(u)) - u
    e = d_hi - d_lo
    b_lo = e - jnp.where(first, 0.0, back(e))
    b_hi = jnp.where(last, 0.0, ahead(e)) - e
    p, q = e - b_lo, b_hi + e
    h = 0.75 * e
    m_lo = (b_lo * b_lo + eps) + h * p
    m_hi = (b_hi * b_hi + eps) + h * q
    s_lo = m_lo + h * (b_lo + b_lo)
    s_hi = m_hi - h * (b_hi + b_hi)
    c_hi = 1.0 / (s_lo * s_lo)
    c_lo = 1.0 / (s_hi * s_hi)
    c = b_hi - b_lo
    k = c + c
    e2 = e + e
    flat = 1.0 / (3.0 * eps * eps)
    a_lo = jnp.where(first, flat, back(c_hi * (1.0 / 3.0)))
    a_hi = jnp.where(last, flat, ahead(c_lo * (1.0 / 3.0)))
    k_lo = jnp.where(first, e2, back(k))
    k_hi = jnp.where(last, e2, ahead(k))
    diff, jump = join(a_lo, 2.0 / (m_lo * m_lo), c_lo, k_lo, a_hi, 2.0 / (m_hi * m_hi), c_hi, k_hi, c)
    return (6.0 * (d_hi + d_lo) - (b_hi + b_lo)) + diff, jump


def iotas():
    shape = (NV, NY)
    row = lax.broadcasted_iota(jnp.int32, shape, 0)
    lane = lax.broadcasted_iota(jnp.int32, shape, 1)
    return row, lane


def speeds_of(row):
    return speed_low + row.astype(jnp.float32) * np.float32(HV)


def pass_vy(u_ref, r_ref, wy_ref, tab_ref, by_ref, pk_ref, lo, hi):
    def body(x, carry):
        row, lane = iotas()
        speeds = speeds_of(row)
        v0, v1 = row == 0, row == NV - 1
        y0, y1 = lane == 0, lane == NY - 1
        wind = wy_ref[x]
        for h in range(NHL):
            u = u_ref[x + 3, h + 3]
            total_v, jump_v = along(u, 0, EPS_V, v0, v1)
            total_y, jump_y = along(u, 1, EPS_X, y0, y1)
            flow = speeds * tab_ref[NHL + h : NHL + h + 1, :] + wind
            rate = total_y * flow + K_V * (jump_v - jnp.abs(total_v))
            if by_ref is not None:
                by_ref[x, h] = jump_y
            else:
                rate = rate + pk_ref[1] * jump_y
            r_ref[x, h] = rate
        return carry

    lax.fori_loop(lo, hi, body, 0)


def pass_h(u_ref, r_ref, lo, hi):
    def body(x, carry):
        for h, (total, jump) in enumerate(line(lambda i: u_ref[x + 3, i + 3], NHL, EPS_T)):
            r_ref[x, h] = r_ref[x, h] + K_T * (jump - jnp.abs(total))
        return carry

    lax.fori_loop(lo, hi, body, 0)


def pass_x(u_ref, wx_ref, tab_ref, lo, finish, group=4):
    def body(t, carry):
        row, _ = iotas()
        speeds = speeds_of(row)
        for j in range(group):
            h = t * group + j
            lanes = speeds * tab_ref[pl.ds(h, 1), :]
            cells = line(lambda i: u_ref[lo + i + 3, h + 3], 3, EPS_X)
            for i, (total, jump) in enumerate(cells):
                finish(lo + i, h, total * (lanes + wx_ref[lo + i]), jump)
        return carry

    lax.fori_loop(0, NHL // group, body, 0)


def bounds():
    speeds = np.float32(speed_low) + np.arange(NV, dtype=np.float32) * np.float32(HV)
    angles = np.arange(NTH, dtype=np.float32) * np.float32(HT)
    px = np.cos(angles)[:, None] * speeds
    py = np.sin(angles)[:, None] * speeds
    return [float(a) for a in (px.max(), -px.min(), py.max(), -py.min())]


def table():
    angles = np.arange(NTH, dtype=np.float32) * np.float32(HT)
    both = np.stack([np.cos(angles).reshape(-1, NHL), np.sin(angles).reshape(-1, NHL)], 1)
    both = both.reshape(NTH // NHL, 2 * NHL, 1).astype(np.float32)
    return np.broadcast_to(both, (NTH // NHL, 2 * NHL, NY)).copy()


def kernel(
    level, wind, mask, depth, tab_all, out,
    u0, u1, u2, r, bx, by, res, wv, mv, dv, tab, wx, wy, tg, pk, pbuf, pmine,
    sem_in, sx, rx, sh, rh, sp, rp, so,
):
    g = lax.axis_index("gx")
    hd = lax.axis_index("head")
    ng, nh = lax.axis_size("gx"), lax.axis_size("head")
    yh, z = g // Z, g % Z
    at = lambda half, z_: half * Z + z_
    across = (hd + nh // 2) % nh
    fields = (u0, u1, u2)

    get_wind = pltpu.make_async_copy(wind, wv, sem_in.at[0])
    get_wind.start()

    barrier = pltpu.get_barrier_semaphore()

    def greet(peer):
        pl.semaphore_signal(barrier, inc=1, device_id=peer, device_id_type=MESH)

    greet({"gx": g, "head": (hd + 1) % nh})
    greet({"gx": g, "head": (hd + nh - 1) % nh})

    @pl.when(g < ng - 1)
    def _():
        greet({"gx": (g + 1) % ng, "head": hd})

    @pl.when(g > 0)
    def _():
        greet({"gx": (g + ng - 1) % ng, "head": hd})

    @pl.when(z == 0)
    def _():
        for i in range(1, Z):
            greet({"gx": at(yh, i), "head": hd})
        for i in range(Z):
            greet({"gx": at(1 - yh, i), "head": across})

    get_level = pltpu.make_async_copy(level, u0.at[pl.ds(3, NXL), pl.ds(3, NHL)], sem_in.at[1])
    get_level.start()
    get_tab = pltpu.make_async_copy(tab_all.at[hd], tab, sem_in.at[2])
    get_tab.start()
    get_mask = pltpu.make_async_copy(mask, mv, sem_in.at[3])
    get_mask.start()
    get_depth = pltpu.make_async_copy(depth, dv, sem_in.at[4])
    get_depth.start()

    get_wind.wait()
    tops = []
    for c in range(2):
        top, low = wv[0, c : c + 1, :], wv[0, c : c + 1, :]
        for i in range(1, NXL):
            top, low = jnp.maximum(top, wv[i, c : c + 1, :]), jnp.minimum(low, wv[i, c : c + 1, :])
        tops += [top, -low]
    row, _ = iotas()
    tile = jnp.broadcast_to(tops[0], (NV, NY))
    for i in range(1, 4):
        tile = jnp.where(row == i, jnp.broadcast_to(tops[i], (NV, NY)), tile)
    pmine[0] = jnp.broadcast_to(jnp.max(tile, axis=1, keepdims=True), (NV, NY))

    def x_copy(s, up):
        src = level if s == 0 else fields[s]
        base = 0 if s == 0 else 3
        start = (NXL - 3 if up else 0) + base
        return pltpu.make_async_remote_copy(
            src_ref=src.at[pl.ds(start, 3), pl.ds(base, NHL)],
            dst_ref=fields[s].at[pl.ds(0 if up else NXL + 3, 3), pl.ds(3, NHL)],
            send_sem=sx.at[s, int(up)],
            recv_sem=rx.at[s, int(up)],
            device_id={"gx": (g + 1) % ng if up else (g + ng - 1) % ng, "head": hd},
            device_id_type=MESH,
        )

    def h_copy(s, up, chunk):
        src = level if s == 0 else fields[s]
        base = 0 if s == 0 else 3
        start = (NHL - 3 if up else 0) + base
        return pltpu.make_async_remote_copy(
            src_ref=src.at[pl.ds(3 * chunk + base, 3), pl.ds(start, 3)],
            dst_ref=fields[s].at[pl.ds(3 * chunk + 3, 3), pl.ds(0 if up else NHL + 3, 3)],
            send_sem=sh.at[s, int(up), chunk],
            recv_sem=rh.at[s, int(up), chunk],
            device_id={"gx": g, "head": (hd + 1) % nh if up else (hd + nh - 1) % nh},
            device_id_type=MESH,
        )

    def send_x(s, up):
        @pl.when(g < ng - 1 if up else g > 0)
        def _():
            x_copy(s, up).start()

    def take_x(s, up):
        @pl.when(g > 0 if up else g < ng - 1)
        def _():
            x_copy(s, up).wait_recv()

        @pl.when(g == 0 if up else g == ng - 1)
        def _():
            for h in range(NHL):
                edge = fields[s][3 if up else NXL + 2, h + 3]
                for i in range(3):
                    fields[s][i if up else NXL + 3 + i, h + 3] = edge

    def send_h(s, chunk):
        for up in (True, False):
            h_copy(s, up, chunk).start()

    def take_h(s, chunk):
        for up in (True, False):
            h_copy(s, up, chunk).wait_recv()

    to_root = lambda: pltpu.make_async_remote_copy(
        src_ref=pmine.at[0], dst_ref=pbuf.at[z], send_sem=sp.at[0], recv_sem=rp.at[z],
        device_id={"gx": at(yh, 0), "head": hd}, device_id_type=MESH,
    )
    to_other = lambda: pltpu.make_async_remote_copy(
        src_ref=pmine.at[0], dst_ref=pbuf.at[Z + z], send_sem=sp.at[1], recv_sem=rp.at[Z + z],
        device_id={"gx": at(1 - yh, 0), "head": across}, device_id_type=MESH,
    )
    answer = lambda i: pltpu.make_async_remote_copy(
        src_ref=pmine.at[1], dst_ref=pbuf.at[2 * Z], send_sem=sp.at[1 + i], recv_sem=rp.at[2 * Z],
        device_id={"gx": at(yh, i), "head": hd}, device_id_type=MESH,
    )
    arrived = lambda slot: pltpu.make_async_remote_copy(
        src_ref=pmine.at[0], dst_ref=pbuf.at[slot], send_sem=sp.at[0], recv_sem=rp.at[slot],
        device_id={"gx": at(1 - yh, 0), "head": across}, device_id_type=MESH,
    )

    greeters = 3 + (g > 0).astype(jnp.int32) + (g < ng - 1).astype(jnp.int32) + (z > 0).astype(jnp.int32)
    pl.semaphore_wait(barrier, greeters)

    @pl.when(z > 0)
    def _():
        to_root().start()

    to_other().start()
    send_x(0, True)
    send_x(0, False)
    for chunk in range(3):
        send_h(0, chunk)

    for i in range(NXL):
        wx[i] = jnp.broadcast_to(wv[i, 0:1, :], (NV, NY))
        wy[i] = jnp.broadcast_to(wv[i, 1:2, :], (NV, NY))
    get_mask.wait()
    get_depth.wait()
    for i in range(NXL):
        d = dv[i : i + 1, :]
        tg[i] = jnp.broadcast_to(jnp.where(mv[i : i + 1, :] == 1, -d, d), (NV, NY))
    get_tab.wait()
    get_level.wait()

    pass_vy(u0, r, wy, tab, by, None, 0, NXL)
    for chunk in range(3):
        take_h(0, chunk)
    pass_h(u0, r, 0, NXL)

    def keep(x, h, part, jump):
        r[x, h] = r[x, h] + part
        bx[x, h] = jump

    def either(low, first, second):
        pl.when(low)(first)
        pl.when(jnp.logical_not(low))(second)

    def both_sides(s, finish, after):
        for low in (g != Z, g == Z):

            @pl.when(low)
            def _():
                take_x(s, True)

            @pl.when(jnp.logical_not(low))
            def _():
                take_x(s, False)

            pass_x(fields[s], wx, tab, jnp.where(low, 0, 6), finish)
            after(low)

    pass_x(u0, wx, tab, 3, keep)
    both_sides(0, keep, lambda low: None)

    @pl.when(z == 0)
    def _():
        best = pmine[0]
        for slot in range(1, 2 * Z):
            arrived(slot).wait_recv()
            best = jnp.maximum(best, pbuf[slot])
        pmine[1] = best
        for i in range(1, Z):
            answer(i).start()

    @pl.when(z > 0)
    def _():
        arrived(2 * Z).wait_recv()
        pmine[1] = pbuf[2 * Z]

    top = pmine[1]
    cx, cnx, cy, cny = bounds()
    peak_x = jnp.maximum(top[0:1] + cx, top[1:2] + cnx)
    peak_y = jnp.maximum(top[2:3] + cy, top[3:4] + cny)
    step = courant / (peak_x / spacing + peak_y / spacing + turn_limit / HT + thrust_limit / HV)
    pk[0] = jnp.broadcast_to(peak_x, (NV, NY))
    pk[1] = jnp.broadcast_to(peak_y, (NV, NY))
    pk[2] = jnp.broadcast_to(step * (1.0 / (12.0 * spacing)), (NV, NY))

    def update_one(lo):
        def body(h, carry):
            px, py, dt = pk[0], pk[1], pk[2]
            for i in range(3):
                rate = r[lo + i, h] + px * bx[lo + i, h] + py * by[lo + i, h]
                u1[lo + i + 3, h + 3] = jnp.minimum(u0[lo + i + 3, h + 3] + dt * rate, tg[lo + i])
            return carry

        lax.fori_loop(0, NHL, body, 0, unroll=2)

    update_one(0)
    send_x(1, False)
    send_h(1, 0)
    update_one(6)
    send_x(1, True)
    send_h(1, 2)
    update_one(3)
    send_h(1, 1)

    def section(s, write, after):
        u = fields[s]
        old, new = (0.75, 0.25) if s == 1 else (1.0 / 3.0, 2.0 / 3.0)
        pass_vy(u, r, wy, tab, None, pk, 0, NXL)
        for chunk in (0, 2, 1):
            take_h(s, chunk)
            pass_h(u, r, 3 * chunk, 3 * chunk + 3)

        def finish(x, h, part, jump):
            rate = (r[x, h] + part) + pk[0] * jump
            now = old * u0[x + 3, h + 3] + new * (u[x + 3, h + 3] + pk[2] * rate)
            write(x, h, jnp.minimum(now, tg[x]))

        pass_x(u, wx, tab, 3, finish)
        after(1)
        both_sides(s, finish, lambda low: either(low, lambda: after(0), lambda: after(2)))

    def write_two(x, h, value):
        u2[x + 3, h + 3] = value

    def after_two(chunk):
        if chunk != 1:
            send_x(2, chunk == 2)
        send_h(2, chunk)

    section(1, write_two, after_two)

    def write_out(x, h, value):
        res[x, h] = value

    puts = [
        pltpu.make_async_copy(res.at[pl.ds(3 * c, 3)], out.at[pl.ds(3 * c, 3)], so.at[c]) for c in range(3)
    ]
    section(2, write_out, lambda chunk: puts[chunk].start())

    for put in puts:
        put.wait()

    @pl.when(z > 0)
    def _():
        to_root().wait_send()

    to_other().wait_send()

    @pl.when(z == 0)
    def _():
        for i in range(1, Z):
            answer(i).wait_send()

    for s in range(3):
        for up in (True, False):

            @pl.when(g < ng - 1 if up else g > 0)
            def _():
                x_copy(s, up).wait_send()

            for chunk in range(3):
                h_copy(s, up, chunk).wait_send()


def local(level_set, wind_field, target_mask, target_depth):
    field = pltpu.VMEM((NXL + 6, NHL + 6, NV, NY), jnp.float32)
    inner = pltpu.VMEM((NXL, NHL, NV, NY), jnp.float32)
    rows = pltpu.VMEM((NXL, NV, NY), jnp.float32)
    dma = pltpu.SemaphoreType.DMA
    inputs = (level_set, jnp.transpose(wind_field, (1, 0, 2)), target_mask, target_depth, jnp.asarray(table()))
    return pl.pallas_call(
        kernel,
        out_shape=jax.ShapeDtypeStruct(level_set.shape, jnp.float32),
        in_specs=[pl.BlockSpec(memory_space=pltpu.HBM)] * 5,
        out_specs=pl.BlockSpec(memory_space=pl.ANY),
        scratch_shapes=[
            field, field, field, inner, inner, inner, inner,
            pltpu.VMEM((NXL, 2, NY), jnp.float32),
            pltpu.VMEM((NXL, NY), jnp.int32),
            pltpu.VMEM((NXL, NY), jnp.float32),
            pltpu.VMEM((2 * NHL, NY), jnp.float32),
            rows, rows, rows,
            pltpu.VMEM((3, NV, NY), jnp.float32),
            pltpu.VMEM((2 * Z + 1, NV, NY), jnp.float32),
            pltpu.VMEM((2, NV, NY), jnp.float32),
            dma((5,)), dma((3, 2)), dma((3, 2)), dma((3, 2, 3)), dma((3, 2, 3)), dma((Z + 1,)), dma((2 * Z + 1,)), dma((3,)),
        ],
        compiler_params=pltpu.CompilerParams(collective_id=0, has_side_effects=True, vmem_limit_bytes=32 * 1024 * 1024),
        name="step",
    )(*[pltpu.with_memory_space_constraint(a, pltpu.HBM) for a in inputs])


def solution(mesh):
    return jax.shard_map(
        local,
        mesh=mesh,
        in_specs=(P("gx", "head", None, None), P(None, "gx", None), P("gx", None), P("gx", None)),
        out_specs=P("gx", "head", None, None),
        check_vma=False,
    )
```

```python
import functools
import math

import jax
import jax.numpy as jnp
import numpy as np
from jax import lax
from jax.experimental import pallas as pl
from jax.experimental.pallas import tpu as pltpu
from jax.sharding import PartitionSpec as P

MESH = pl.DeviceIdType.MESH
epsilon = 1e-06
courant = 0.5
spacing = 0.05
turn_limit = 1.0
thrust_limit = 0.5
speed_low = 0.5
speed_high = 1.5
NV = 8
NY = 128
NX = 288
NTH = 192
NXL = 9
NHL = 12
HT = 2.0 * math.pi / NTH
HV = (speed_high - speed_low) / (NV - 1)
EPS_X = 0.75 * epsilon * spacing**2
EPS_T = 0.75 * epsilon * HT**2
EPS_V = 0.75 * epsilon * HV**2
K_T = turn_limit * spacing / HT
K_V = thrust_limit * spacing / HV
Z = 16


def face(p, q, hp, hq, eps, left, mid, right):
    b = q - p
    b2 = b + b
    smooth = (b * b + eps) + hp * q
    out = {"b2": b2}
    if left:
        s = smooth + hq * b2
        out["L"] = 1.0 / (s * s)
        out["aL"] = out["L"] * (1.0 / 3.0)
    if mid:
        out["M"] = 2.0 / (smooth * smooth)
    if right:
        s = smooth - hp * b2
        out["R"] = 1.0 / (s * s)
        out["aR"] = out["R"] * (1.0 / 3.0)
    return out


def join(a_lo, m_lo, c_lo, k_lo, a_hi, m_hi, c_hi, k_hi, c):
    low = (a_lo * k_lo + c_lo * c) / ((a_lo + c_lo) + m_lo)
    high = (a_hi * k_hi + c_hi * c) / ((a_hi + c_hi) + m_hi)
    return high - low, (high + low) - c


def line(load, n, eps):
    u = {i: load(i) for i in range(-3, n + 3)}
    d = {i: u[i + 1] - u[i] for i in range(-3, n + 2)}
    e = {i: d[i] - d[i - 1] for i in range(-2, n + 2)}
    h = {i: 0.75 * e[i] for i in e}
    f = {
        i: face(e[i], e[i + 1], h[i], h[i + 1], eps, i <= n - 2, -1 <= i <= n - 1, i >= 0)
        for i in range(-2, n + 1)
    }
    k = {i: f[i]["b2"] - f[i - 1]["b2"] for i in range(-1, n + 1)}
    g = {i: 6.0 * u[i] - e[i] for i in range(-1, n + 1)}
    return finished(f, k, g, n)


def along(u, axis, eps, first, last):
    n = u.shape[axis]
    back = lambda a: pltpu.roll(a, 1, axis)
    ahead = lambda a: pltpu.roll(a, n - 1, axis)
    d_lo = u - jnp.where(first, u, back(u))
    d_hi = jnp.where(last, u, ahead(u)) - u
    e = d_hi - d_lo
    b_lo = e - jnp.where(first, 0.0, back(e))
    b_hi = jnp.where(last, 0.0, ahead(e)) - e
    p, q = e - b_lo, b_hi + e
    h = 0.75 * e
    m_lo = (b_lo * b_lo + eps) + h * p
    m_hi = (b_hi * b_hi + eps) + h * q
    s_lo = m_lo + h * (b_lo + b_lo)
    s_hi = m_hi - h * (b_hi + b_hi)
    c_hi = 1.0 / (s_lo * s_lo)
    c_lo = 1.0 / (s_hi * s_hi)
    c = b_hi - b_lo
    k = c + c
    e2 = e + e
    flat = 1.0 / (3.0 * eps * eps)
    a_lo = jnp.where(first, flat, back(c_hi * (1.0 / 3.0)))
    a_hi = jnp.where(last, flat, ahead(c_lo * (1.0 / 3.0)))
    k_lo = jnp.where(first, e2, back(k))
    k_hi = jnp.where(last, e2, ahead(k))
    diff, jump = join(a_lo, 2.0 / (m_lo * m_lo), c_lo, k_lo, a_hi, 2.0 / (m_hi * m_hi), c_hi, k_hi, c)
    return (6.0 * (d_hi + d_lo) - (b_hi + b_lo)) + diff, jump


def closed(load, n, eps):
    u = [load(i) for i in range(n)]
    d = [u[i + 1] - u[i] for i in range(n - 1)]
    e = [d[0]] + [d[i] - d[i - 1] for i in range(1, n - 1)] + [-d[n - 2]]
    h = [0.75 * a for a in e]
    f = {i: face(e[i], e[i + 1], h[i], h[i + 1], eps, True, True, True) for i in range(n - 1)}
    twice = [e[0] + e[0], e[n - 1] + e[n - 1]]
    rim = [e[0] * e[0] + eps, e[n - 1] * e[n - 1] + eps]
    out_l, out_r = rim[0] + h[0] * twice[0], rim[1] + h[n - 1] * twice[1]
    left, right = 1.0 / (out_l * out_l), 1.0 / (out_r * out_r)
    flat = 1.0 / (3.0 * eps * eps)
    f[-2], f[n] = {"aL": flat}, {"aR": flat}
    f[-1] = {"b2": twice[0], "L": left, "aL": left * (1.0 / 3.0), "M": 2.0 / (rim[0] * rim[0])}
    f[n - 1] = {"b2": -twice[1], "R": right, "aR": right * (1.0 / 3.0), "M": 2.0 / (rim[1] * rim[1])}
    k = {i: f[i]["b2"] - f[i - 1]["b2"] for i in range(n)}
    k[-1], k[n] = twice
    u6 = [6.0 * a for a in u]
    g = {i: u6[i] - e[i] for i in range(n)}
    g[-1], g[n] = u6[0], u6[n - 1]
    return finished(f, k, g, n)


def finished(f, k, g, n):
    result = []
    for i in range(n):
        diff, jump = join(
            f[i - 2]["aL"], f[i - 1]["M"], f[i]["R"], k[i - 1],
            f[i + 1]["aR"], f[i]["M"], f[i - 1]["L"], k[i + 1],
            0.5 * k[i],
        )
        result.append(((g[i + 1] - g[i - 1]) + diff, jump))
    return result


def iotas():
    shape = (NV, NY)
    row = lax.broadcasted_iota(jnp.int32, shape, 0)
    lane = lax.broadcasted_iota(jnp.int32, shape, 1)
    return row, lane


def speeds_of(row):
    return speed_low + row.astype(jnp.float32) * np.float32(HV)


def pass_vy(u_ref, v_ref, r_ref, wy_ref, tab_ref, by_ref, pk_ref):
    wide = NHL + 6
    u_rows = u_ref.reshape((NXL + 6) * wide * NV, NY)
    r_rows = v_ref.reshape(NXL * NHL * NV, NY)

    def speed_terms(x, h, along_x):
        u_at = ((x + 3) * wide + h + 3) * NV
        r_at = (x * NHL + h) * NV
        u_step, r_step = (wide * NV, NHL * NV) if along_x else (NV, NV)
        cells = closed(lambda v: u_rows[pl.ds(u_at + v, 8, stride=u_step), :], NV, EPS_V)
        for v, (total, jump) in enumerate(cells):
            r_rows[pl.ds(r_at + v, 8, stride=r_step), :] = K_V * (jump - jnp.abs(total))

    def y_terms(cells):
        row, lane = iotas()
        speeds = speeds_of(row)
        y0, y1 = lane == 0, lane == NY - 1
        for x, h in cells:
            total, jump = along(u_ref[x + 3, h + 3], 1, EPS_X, y0, y1)
            rate = total * (speeds * tab_ref[pl.ds(NHL + h, 1), :] + wy_ref[x])
            if by_ref is not None:
                by_ref[x, h] = jump
            else:
                rate = rate + pk_ref[1] * jump
            r_ref[x, h] = rate

    def body(t, carry):
        for j in range(3):
            y_terms([(x, 3 * t + j) for x in range(8)])
            speed_terms(0, 3 * t + j, True)
        return carry

    lax.fori_loop(0, NHL // 3, body, 0)
    for x in range(8, NXL):
        for h in (0, NHL - 8):
            speed_terms(x, h, False)
        y_terms([(x, h) for h in range(NHL)])


def pass_h(u_ref, lo, hi, finish):
    def body(x, carry):
        for h, (total, jump) in enumerate(line(lambda i: u_ref[x + 3, i + 3], NHL, EPS_T)):
            finish(x, h, K_T * (jump - jnp.abs(total)))
        return carry

    lax.fori_loop(lo, hi, body, 0)


def pass_x(u_ref, wx_ref, tab_ref, lo, planes, group, finish):
    def body(t, carry):
        row, _ = iotas()
        speeds = speeds_of(row)
        for j in range(group):
            h = t * group + j
            lanes = speeds * tab_ref[pl.ds(h, 1), :]
            cells = line(lambda i: u_ref[lo + i + 3, h + 3], planes, EPS_X)
            for i, (total, jump) in enumerate(cells):
                finish(lo + i, h, total * (lanes + wx_ref[lo + i]), jump)
        return carry

    if group == NHL:
        body(0, 0)
    else:
        lax.fori_loop(0, NHL // group, body, 0)


def bounds():
    speeds = np.float32(speed_low) + np.arange(NV, dtype=np.float32) * np.float32(HV)
    angles = np.arange(NTH, dtype=np.float32) * np.float32(HT)
    px = np.cos(angles)[:, None] * speeds
    py = np.sin(angles)[:, None] * speeds
    return [float(a) for a in (px.max(), -px.min(), py.max(), -py.min())]


def table():
    angles = np.arange(NTH, dtype=np.float32) * np.float32(HT)
    both = np.stack([np.cos(angles).reshape(-1, NHL), np.sin(angles).reshape(-1, NHL)], 1)
    both = both.reshape(NTH // NHL, 2 * NHL, 1).astype(np.float32)
    return np.broadcast_to(both, (NTH // NHL, 2 * NHL, NY)).copy()


def kernel(
    level, wind, mask, depth, tab_all, out,
    u0, u1, u2, r, rv, bx, by, res, wv, mv, dv, tab, wx, wy, tg, pk, pbuf, pmine,
    sem_in, sx, rx, sh, rh, sp, rp, so,
):
    g = lax.axis_index("gx")
    hd = lax.axis_index("head")
    ng, nh = lax.axis_size("gx"), lax.axis_size("head")
    yh, z = g // Z, g % Z
    at = lambda half, z_: half * Z + z_
    across = (hd + nh // 2) % nh
    fields = (u0, u1, u2)

    get_wind = pltpu.make_async_copy(wind, wv, sem_in.at[0])
    get_wind.start()

    barrier = pltpu.get_barrier_semaphore()

    def greet(peer):
        pl.semaphore_signal(barrier, inc=1, device_id=peer, device_id_type=MESH)

    greet({"gx": g, "head": (hd + 1) % nh})
    greet({"gx": g, "head": (hd + nh - 1) % nh})

    @pl.when(g < ng - 1)
    def _():
        greet({"gx": (g + 1) % ng, "head": hd})

    @pl.when(g > 0)
    def _():
        greet({"gx": (g + ng - 1) % ng, "head": hd})

    @pl.when(z == 0)
    def _():
        for i in range(1, Z):
            greet({"gx": at(yh, i), "head": hd})
        for i in range(Z):
            greet({"gx": at(1 - yh, i), "head": across})

    get_level = pltpu.make_async_copy(level, u0.at[pl.ds(3, NXL), pl.ds(3, NHL)], sem_in.at[1])
    get_level.start()
    get_tab = pltpu.make_async_copy(tab_all.at[hd], tab, sem_in.at[2])
    get_tab.start()
    get_mask = pltpu.make_async_copy(mask, mv, sem_in.at[3])
    get_mask.start()
    get_depth = pltpu.make_async_copy(depth, dv, sem_in.at[4])
    get_depth.start()

    get_wind.wait()
    tops = []
    for c in range(2):
        top, low = wv[0, c : c + 1, :], wv[0, c : c + 1, :]
        for i in range(1, NXL):
            top, low = jnp.maximum(top, wv[i, c : c + 1, :]), jnp.minimum(low, wv[i, c : c + 1, :])
        tops += [top, -low]
    row, _ = iotas()
    tile = jnp.broadcast_to(tops[0], (NV, NY))
    for i in range(1, 4):
        tile = jnp.where(row == i, jnp.broadcast_to(tops[i], (NV, NY)), tile)
    pmine[0] = jnp.broadcast_to(jnp.max(tile, axis=1, keepdims=True), (NV, NY))

    def x_copy(s, up):
        src = level if s == 0 else fields[s]
        base = 0 if s == 0 else 3
        start = (NXL - 3 if up else 0) + base
        return pltpu.make_async_remote_copy(
            src_ref=src.at[pl.ds(start, 3), pl.ds(base, NHL)],
            dst_ref=fields[s].at[pl.ds(0 if up else NXL + 3, 3), pl.ds(3, NHL)],
            send_sem=sx.at[s, int(up)],
            recv_sem=rx.at[s, int(up)],
            device_id={"gx": (g + 1) % ng if up else (g + ng - 1) % ng, "head": hd},
            device_id_type=MESH,
        )

    def h_copy(s, up, chunk):
        src = level if s == 0 else fields[s]
        base = 0 if s == 0 else 3
        start = (NHL - 3 if up else 0) + base
        return pltpu.make_async_remote_copy(
            src_ref=src.at[pl.ds(3 * chunk + base, 3), pl.ds(start, 3)],
            dst_ref=fields[s].at[pl.ds(3 * chunk + 3, 3), pl.ds(0 if up else NHL + 3, 3)],
            send_sem=sh.at[s, int(up), chunk],
            recv_sem=rh.at[s, int(up), chunk],
            device_id={"gx": g, "head": (hd + 1) % nh if up else (hd + nh - 1) % nh},
            device_id_type=MESH,
        )

    def send_x(s, up):
        @pl.when(g < ng - 1 if up else g > 0)
        def _():
            x_copy(s, up).start()

    def take_x(s, up):
        @pl.when(g > 0 if up else g < ng - 1)
        def _():
            x_copy(s, up).wait_recv()

        @pl.when(g == 0 if up else g == ng - 1)
        def _():
            for h in range(NHL):
                edge = fields[s][3 if up else NXL + 2, h + 3]
                for i in range(3):
                    fields[s][i if up else NXL + 3 + i, h + 3] = edge

    def send_h(s, chunk):
        for up in (True, False):
            h_copy(s, up, chunk).start()

    def take_h(s, chunk):
        for up in (True, False):
            h_copy(s, up, chunk).wait_recv()

    to_root = lambda: pltpu.make_async_remote_copy(
        src_ref=pmine.at[0, pl.ds(0, 4)], dst_ref=pbuf.at[z, pl.ds(0, 4)], send_sem=sp.at[0], recv_sem=rp.at[z],
        device_id={"gx": at(yh, 0), "head": hd}, device_id_type=MESH,
    )
    to_other = lambda: pltpu.make_async_remote_copy(
        src_ref=pmine.at[0, pl.ds(0, 4)], dst_ref=pbuf.at[Z + z, pl.ds(0, 4)], send_sem=sp.at[1], recv_sem=rp.at[Z + z],
        device_id={"gx": at(1 - yh, 0), "head": across}, device_id_type=MESH,
    )
    answer = lambda i: pltpu.make_async_remote_copy(
        src_ref=pmine.at[1, pl.ds(0, 4)], dst_ref=pbuf.at[2 * Z, pl.ds(0, 4)], send_sem=sp.at[1 + i], recv_sem=rp.at[2 * Z],
        device_id={"gx": at(yh, i), "head": hd}, device_id_type=MESH,
    )
    arrived = lambda slot: pltpu.make_async_remote_copy(
        src_ref=pmine.at[0, pl.ds(0, 4)], dst_ref=pbuf.at[slot, pl.ds(0, 4)], send_sem=sp.at[0], recv_sem=rp.at[slot],
        device_id={"gx": at(1 - yh, 0), "head": across}, device_id_type=MESH,
    )

    greeters = 3 + (g > 0).astype(jnp.int32) + (g < ng - 1).astype(jnp.int32) + (z > 0).astype(jnp.int32)
    pl.semaphore_wait(barrier, greeters)

    @pl.when(z > 0)
    def _():
        to_root().start()

    to_other().start()
    send_x(0, True)
    send_x(0, False)
    for chunk in range(3):
        send_h(0, chunk)

    for i in range(NXL):
        wx[i] = jnp.broadcast_to(wv[i, 0:1, :], (NV, NY))
        wy[i] = jnp.broadcast_to(wv[i, 1:2, :], (NV, NY))
    get_mask.wait()
    get_depth.wait()
    for i in range(NXL):
        d = dv[i : i + 1, :]
        tg[i] = jnp.broadcast_to(jnp.where(mv[i : i + 1, :] == 1, -d, d), (NV, NY))
    get_tab.wait()
    get_level.wait()

    pass_vy(u0, rv, r, wy, tab, by, None)
    for chunk in range(3):
        take_h(0, chunk)
    def add(x, h, part):
        r[x, h] = (r[x, h] + rv[x, h]) + part

    pass_h(u0, 0, NXL, add)

    def keep(x, h, part, jump):
        r[x, h] = r[x, h] + part
        bx[x, h] = jump

    def either(low, first, second):
        pl.when(low)(first)
        pl.when(jnp.logical_not(low))(second)

    def both_sides(s, finish, after):
        usual = jnp.logical_and(g != Z, g != Z - 1)
        for low in (usual, jnp.logical_not(usual)):
            either(low, lambda: take_x(s, True), lambda: take_x(s, False))
            pass_x(fields[s], wx, tab, jnp.where(low, 0, 6), 3, 4, finish)
            either(low, lambda: after(0), lambda: after(2))

    pass_x(u0, wx, tab, 3, 3, 4, keep)
    both_sides(0, keep, lambda chunk: None)

    @pl.when(z == 0)
    def _():
        best = pmine[0, 0:4]
        for slot in range(1, 2 * Z):
            arrived(slot).wait_recv()
            best = jnp.maximum(best, pbuf[slot, 0:4])
        pmine[1, 0:4] = best
        for i in range(1, Z):
            answer(i).start()

    @pl.when(z > 0)
    def _():
        arrived(2 * Z).wait_recv()
        pmine[1, 0:4] = pbuf[2 * Z, 0:4]

    top = pmine[1, 0:4]
    cx, cnx, cy, cny = bounds()
    peak_x = jnp.maximum(top[0:1] + cx, top[1:2] + cnx)
    peak_y = jnp.maximum(top[2:3] + cy, top[3:4] + cny)
    step = courant / (peak_x / spacing + peak_y / spacing + turn_limit / HT + thrust_limit / HV)
    pk[0] = jnp.broadcast_to(peak_x, (NV, NY))
    pk[1] = jnp.broadcast_to(peak_y, (NV, NY))
    pk[2] = jnp.broadcast_to(step * (1.0 / (12.0 * spacing)), (NV, NY))

    def update_one(lo):
        def body(h, carry):
            px, py, dt = pk[0], pk[1], pk[2]
            for i in range(3):
                rate = r[lo + i, h] + px * bx[lo + i, h] + py * by[lo + i, h]
                u1[lo + i + 3, h + 3] = jnp.minimum(u0[lo + i + 3, h + 3] + dt * rate, tg[lo + i])
            return carry

        lax.fori_loop(0, NHL, body, 0, unroll=2)

    update_one(0)
    send_x(1, False)
    send_h(1, 0)
    update_one(6)
    send_x(1, True)
    send_h(1, 2)
    update_one(3)
    send_h(1, 1)

    def section(s, write, after):
        u = fields[s]
        old, new = (0.75, 0.25) if s == 1 else (1.0 / 3.0, 2.0 / 3.0)
        pass_vy(u, rv, r, wy, tab, None, pk)

        def join_x(x, h, part, jump):
            r[x, h] = (r[x, h] + part) + pk[0] * jump

        def close(x, h, rate):
            now = old * u0[x + 3, h + 3] + new * (u[x + 3, h + 3] + pk[2] * rate)
            write(x, h, jnp.minimum(now, tg[x]))

        def finish_x(x, h, part, jump):
            close(x, h, (r[x, h] + part) + pk[0] * jump)

        def finish_h(x, h, part):
            close(x, h, (r[x, h] + rv[x, h]) + part)

        def middle():
            take_h(s, 1)
            pass_h(u, 3, 6, finish_h)
            after(1)

        pass_x(u, wx, tab, 3, 3, 4, join_x)
        for chunk in (0, 2):
            take_h(s, chunk)
            pass_h(u, 3 * chunk, 3 * chunk + 3, add)
        if s == 2:
            middle()
        else:
            pl.when(g == Z)(middle)
        both_sides(s, finish_x, after)
        if s == 1:
            pl.when(g != Z)(middle)

    def write_two(x, h, value):
        u2[x + 3, h + 3] = value

    def after_two(chunk):
        if chunk != 1:
            send_x(2, chunk == 2)
        send_h(2, chunk)

    section(1, write_two, after_two)

    def write_out(x, h, value):
        res[x, h] = value

    puts = [
        pltpu.make_async_copy(res.at[pl.ds(3 * c, 3)], out.at[pl.ds(3 * c, 3)], so.at[c]) for c in range(3)
    ]
    section(2, write_out, lambda chunk: puts[chunk].start())

    for put in puts:
        put.wait()

    @pl.when(z > 0)
    def _():
        to_root().wait_send()

    to_other().wait_send()

    @pl.when(z == 0)
    def _():
        for i in range(1, Z):
            answer(i).wait_send()

    for s in range(3):
        for up in (True, False):

            @pl.when(g < ng - 1 if up else g > 0)
            def _():
                x_copy(s, up).wait_send()

            for chunk in range(3):
                h_copy(s, up, chunk).wait_send()


def local(level_set, wind_field, target_mask, target_depth):
    field = pltpu.VMEM((NXL + 6, NHL + 6, NV, NY), jnp.float32)
    inner = pltpu.VMEM((NXL, NHL, NV, NY), jnp.float32)
    rows = pltpu.VMEM((NXL, NV, NY), jnp.float32)
    dma = pltpu.SemaphoreType.DMA
    inputs = (level_set, jnp.transpose(wind_field, (1, 0, 2)), target_mask, target_depth, jnp.asarray(table()))
    return pl.pallas_call(
        kernel,
        out_shape=jax.ShapeDtypeStruct(level_set.shape, jnp.float32),
        in_specs=[pl.BlockSpec(memory_space=pltpu.HBM)] * 5,
        out_specs=pl.BlockSpec(memory_space=pl.ANY),
        scratch_shapes=[
            field, field, field, inner, inner, inner, inner, inner,
            pltpu.VMEM((NXL, 2, NY), jnp.float32),
            pltpu.VMEM((NXL, NY), jnp.int32),
            pltpu.VMEM((NXL, NY), jnp.float32),
            pltpu.VMEM((2 * NHL, NY), jnp.float32),
            rows, rows, rows,
            pltpu.VMEM((3, NV, NY), jnp.float32),
            pltpu.VMEM((2 * Z + 1, NV, NY), jnp.float32),
            pltpu.VMEM((2, NV, NY), jnp.float32),
            dma((5,)), dma((3, 2)), dma((3, 2)), dma((3, 2, 3)), dma((3, 2, 3)), dma((Z + 1,)), dma((2 * Z + 1,)), dma((3,)),
        ],
        compiler_params=pltpu.CompilerParams(collective_id=0, has_side_effects=True, vmem_limit_bytes=32 * 1024 * 1024),
        name="step",
    )(*[pltpu.with_memory_space_constraint(a, pltpu.HBM) for a in inputs])


def solution(mesh):
    return jax.shard_map(
        local,
        mesh=mesh,
        in_specs=(P("gx", "head", None, None), P(None, "gx", None), P("gx", None), P("gx", None)),
        out_specs=P("gx", "head", None, None),
        check_vma=False,
    )
```

```python
import functools
import math

import jax
import jax.numpy as jnp
import numpy as np
from jax import lax
from jax.experimental import pallas as pl
from jax.experimental.pallas import tpu as pltpu
from jax.sharding import PartitionSpec as P

MESH = pl.DeviceIdType.MESH
epsilon = 1e-06
courant = 0.5
spacing = 0.05
turn_limit = 1.0
thrust_limit = 0.5
speed_low = 0.5
speed_high = 1.5
NV = 8
NY = 128
NX = 288
NTH = 192
NXL = 9
NHL = 12
HT = 2.0 * math.pi / NTH
HV = (speed_high - speed_low) / (NV - 1)
EPS_X = 0.75 * epsilon * spacing**2
EPS_T = 0.75 * epsilon * HT**2
EPS_V = 0.75 * epsilon * HV**2
K_T = turn_limit * spacing / HT
K_V = thrust_limit * spacing / HV
Z = 16


def face(p, q, hp, hq, eps, left, mid, right):
    b = q - p
    b2 = b + b
    smooth = (b * b + eps) + hp * q
    out = {"b2": b2}
    if left:
        s = smooth + hq * b2
        out["L"] = 1.0 / (s * s)
        out["aL"] = out["L"] * (1.0 / 3.0)
    if mid:
        out["M"] = 2.0 / (smooth * smooth)
    if right:
        s = smooth - hp * b2
        out["R"] = 1.0 / (s * s)
        out["aR"] = out["R"] * (1.0 / 3.0)
    return out


def join(a_lo, m_lo, c_lo, k_lo, a_hi, m_hi, c_hi, k_hi, c):
    low = (a_lo * k_lo + c_lo * c) / ((a_lo + c_lo) + m_lo)
    high = (a_hi * k_hi + c_hi * c) / ((a_hi + c_hi) + m_hi)
    return high - low, (high + low) - c


def line(load, n, eps):
    u = {i: load(i) for i in range(-3, n + 3)}
    d = {i: u[i + 1] - u[i] for i in range(-3, n + 2)}
    e = {i: d[i] - d[i - 1] for i in range(-2, n + 2)}
    h = {i: 0.75 * e[i] for i in e}
    f = {
        i: face(e[i], e[i + 1], h[i], h[i + 1], eps, i <= n - 2, -1 <= i <= n - 1, i >= 0)
        for i in range(-2, n + 1)
    }
    k = {i: f[i]["b2"] - f[i - 1]["b2"] for i in range(-1, n + 1)}
    g = {i: 6.0 * u[i] - e[i] for i in range(-1, n + 1)}
    return finished(f, k, g, n)


def along(u, axis, eps, first, last):
    n = u.shape[axis]
    back = lambda a: pltpu.roll(a, 1, axis)
    ahead = lambda a: pltpu.roll(a, n - 1, axis)
    d_lo = u - jnp.where(first, u, back(u))
    d_hi = jnp.where(last, u, ahead(u)) - u
    e = d_hi - d_lo
    b_lo = e - jnp.where(first, 0.0, back(e))
    b_hi = jnp.where(last, 0.0, ahead(e)) - e
    p, q = e - b_lo, b_hi + e
    h = 0.75 * e
    m_lo = (b_lo * b_lo + eps) + h * p
    m_hi = (b_hi * b_hi + eps) + h * q
    s_lo = m_lo + h * (b_lo + b_lo)
    s_hi = m_hi - h * (b_hi + b_hi)
    c_hi = 1.0 / (s_lo * s_lo)
    c_lo = 1.0 / (s_hi * s_hi)
    c = b_hi - b_lo
    k = c + c
    e2 = e + e
    flat = 1.0 / (3.0 * eps * eps)
    a_lo = jnp.where(first, flat, back(c_hi * (1.0 / 3.0)))
    a_hi = jnp.where(last, flat, ahead(c_lo * (1.0 / 3.0)))
    k_lo = jnp.where(first, e2, back(k))
    k_hi = jnp.where(last, e2, ahead(k))
    diff, jump = join(a_lo, 2.0 / (m_lo * m_lo), c_lo, k_lo, a_hi, 2.0 / (m_hi * m_hi), c_hi, k_hi, c)
    return (6.0 * (d_hi + d_lo) - (b_hi + b_lo)) + diff, jump


def closed(load, n, eps):
    u = [load(i) for i in range(n)]
    d = [u[i + 1] - u[i] for i in range(n - 1)]
    e = [d[0]] + [d[i] - d[i - 1] for i in range(1, n - 1)] + [-d[n - 2]]
    h = [0.75 * a for a in e]
    f = {i: face(e[i], e[i + 1], h[i], h[i + 1], eps, True, True, True) for i in range(n - 1)}
    twice = [e[0] + e[0], e[n - 1] + e[n - 1]]
    rim = [e[0] * e[0] + eps, e[n - 1] * e[n - 1] + eps]
    out_l, out_r = rim[0] + h[0] * twice[0], rim[1] + h[n - 1] * twice[1]
    left, right = 1.0 / (out_l * out_l), 1.0 / (out_r * out_r)
    flat = 1.0 / (3.0 * eps * eps)
    f[-2], f[n] = {"aL": flat}, {"aR": flat}
    f[-1] = {"b2": twice[0], "L": left, "aL": left * (1.0 / 3.0), "M": 2.0 / (rim[0] * rim[0])}
    f[n - 1] = {"b2": -twice[1], "R": right, "aR": right * (1.0 / 3.0), "M": 2.0 / (rim[1] * rim[1])}
    k = {i: f[i]["b2"] - f[i - 1]["b2"] for i in range(n)}
    k[-1], k[n] = twice
    u6 = [6.0 * a for a in u]
    g = {i: u6[i] - e[i] for i in range(n)}
    g[-1], g[n] = u6[0], u6[n - 1]
    return finished(f, k, g, n)


def finished(f, k, g, n):
    result = []
    for i in range(n):
        diff, jump = join(
            f[i - 2]["aL"], f[i - 1]["M"], f[i]["R"], k[i - 1],
            f[i + 1]["aR"], f[i]["M"], f[i - 1]["L"], k[i + 1],
            0.5 * k[i],
        )
        result.append(((g[i + 1] - g[i - 1]) + diff, jump))
    return result


def iotas():
    shape = (NV, NY)
    row = lax.broadcasted_iota(jnp.int32, shape, 0)
    lane = lax.broadcasted_iota(jnp.int32, shape, 1)
    return row, lane


def speeds_of(row):
    return speed_low + row.astype(jnp.float32) * np.float32(HV)


def pass_vy(u_ref, v_ref, r_ref, wx_ref, wy_ref, tab_ref, bx_ref, by_ref, pk_ref):
    wide = NHL + 6
    u_rows = u_ref.reshape((NXL + 6) * wide * NV, NY)
    r_rows = v_ref.reshape(NXL * NHL * NV, NY)

    def speed_terms(x, h, along_x):
        u_at = ((x + 3) * wide + h + 3) * NV
        r_at = (x * NHL + h) * NV
        u_step, r_step = (wide * NV, NHL * NV) if along_x else (NV, NV)
        cells = closed(lambda v: u_rows[pl.ds(u_at + v, 8, stride=u_step), :], NV, EPS_V)
        for v, (total, jump) in enumerate(cells):
            r_rows[pl.ds(r_at + v, 8, stride=r_step), :] = K_V * (jump - jnp.abs(total))

    def y_terms(cells, extra={}):
        row, lane = iotas()
        speeds = speeds_of(row)
        y0, y1 = lane == 0, lane == NY - 1
        for x, h in cells:
            total, jump = along(u_ref[x + 3, h + 3], 1, EPS_X, y0, y1)
            rate = total * (speeds * tab_ref[pl.ds(NHL + h, 1), :] + wy_ref[x])
            if x in extra:
                rate = rate + extra[x]
            if by_ref is not None:
                by_ref[x, h] = jump
            else:
                rate = rate + pk_ref[1] * jump
            r_ref[x, h] = rate

    def middle_terms(h):
        row, _ = iotas()
        lanes = speeds_of(row) * tab_ref[pl.ds(h, 1), :]
        parts = {}
        for i, (total, jump) in enumerate(line(lambda i: u_ref[i + 6, h + 3], 3, EPS_X)):
            parts[3 + i] = total * (lanes + wx_ref[3 + i])
            if bx_ref is not None:
                bx_ref[3 + i, h] = jump
            else:
                parts[3 + i] = parts[3 + i] + pk_ref[0] * jump
        return parts

    def body(t, carry):
        for j in range(3):
            h = 3 * t + j
            y_terms([(x, h) for x in range(8)], middle_terms(h))
            speed_terms(0, h, True)
        return carry

    lax.fori_loop(0, NHL // 3, body, 0)
    for x in range(8, NXL):
        for h in (0, NHL - 8):
            speed_terms(x, h, False)
        y_terms([(x, h) for h in range(NHL)])


def pass_h(u_ref, lo, hi, finish):
    def body(x, carry):
        for h, (total, jump) in enumerate(line(lambda i: u_ref[x + 3, i + 3], NHL, EPS_T)):
            finish(x, h, K_T * (jump - jnp.abs(total)))
        return carry

    lax.fori_loop(lo, hi, body, 0)


def pass_x(u_ref, wx_ref, tab_ref, lo, planes, group, finish):
    def body(t, carry):
        row, _ = iotas()
        speeds = speeds_of(row)
        for j in range(group):
            h = t * group + j
            lanes = speeds * tab_ref[pl.ds(h, 1), :]
            cells = line(lambda i: u_ref[lo + i + 3, h + 3], planes, EPS_X)
            for i, (total, jump) in enumerate(cells):
                finish(lo + i, h, total * (lanes + wx_ref[lo + i]), jump)
        return carry

    if group == NHL:
        body(0, 0)
    else:
        lax.fori_loop(0, NHL // group, body, 0)


def bounds():
    speeds = np.float32(speed_low) + np.arange(NV, dtype=np.float32) * np.float32(HV)
    angles = np.arange(NTH, dtype=np.float32) * np.float32(HT)
    px = np.cos(angles)[:, None] * speeds
    py = np.sin(angles)[:, None] * speeds
    return [float(a) for a in (px.max(), -px.min(), py.max(), -py.min())]


def table():
    angles = np.arange(NTH, dtype=np.float32) * np.float32(HT)
    both = np.stack([np.cos(angles).reshape(-1, NHL), np.sin(angles).reshape(-1, NHL)], 1)
    both = both.reshape(NTH // NHL, 2 * NHL, 1).astype(np.float32)
    return np.broadcast_to(both, (NTH // NHL, 2 * NHL, NY)).copy()


def kernel(
    level, wind, mask, depth, tab_all, out,
    u0, u1, u2, r, rv, bx, by, wv, mv, dv, tab, wx, wy, tg, pk, pbuf, pmine,
    sem_in, sx, rx, sh, rh, sp, rp,
):
    g = lax.axis_index("gx")
    hd = lax.axis_index("head")
    ng, nh = lax.axis_size("gx"), lax.axis_size("head")
    yh, z = g // Z, g % Z
    at = lambda half, z_: half * Z + z_
    across = (hd + nh // 2) % nh
    fields = (u0, u1, u2)

    get_wind = pltpu.make_async_copy(wind, wv, sem_in.at[0])
    get_wind.start()

    barrier = pltpu.get_barrier_semaphore()

    def greet(peer):
        pl.semaphore_signal(barrier, inc=1, device_id=peer, device_id_type=MESH)

    greet({"gx": g, "head": (hd + 1) % nh})
    greet({"gx": g, "head": (hd + nh - 1) % nh})

    @pl.when(g < ng - 1)
    def _():
        greet({"gx": (g + 1) % ng, "head": hd})

    @pl.when(g > 0)
    def _():
        greet({"gx": (g + ng - 1) % ng, "head": hd})

    @pl.when(z == 0)
    def _():
        for i in range(1, Z):
            greet({"gx": at(yh, i), "head": hd})
        for i in range(Z):
            greet({"gx": at(1 - yh, i), "head": across})

    get_level = pltpu.make_async_copy(level, u0.at[pl.ds(3, NXL), pl.ds(3, NHL)], sem_in.at[1])
    get_level.start()
    get_tab = pltpu.make_async_copy(tab_all.at[hd], tab, sem_in.at[2])
    get_tab.start()
    get_mask = pltpu.make_async_copy(mask, mv, sem_in.at[3])
    get_mask.start()
    get_depth = pltpu.make_async_copy(depth, dv, sem_in.at[4])
    get_depth.start()

    get_wind.wait()
    tops = []
    for c in range(2):
        top, low = wv[0, c : c + 1, :], wv[0, c : c + 1, :]
        for i in range(1, NXL):
            top, low = jnp.maximum(top, wv[i, c : c + 1, :]), jnp.minimum(low, wv[i, c : c + 1, :])
        tops += [top, -low]
    row, _ = iotas()
    tile = jnp.broadcast_to(tops[0], (NV, NY))
    for i in range(1, 4):
        tile = jnp.where(row == i, jnp.broadcast_to(tops[i], (NV, NY)), tile)
    pmine[0] = jnp.broadcast_to(jnp.max(tile, axis=1, keepdims=True), (NV, NY))

    def x_copy(s, up, k):
        src = level if s == 0 else fields[s]
        base = 0 if s == 0 else 3
        return pltpu.make_async_remote_copy(
            src_ref=src.at[(NXL - 1 - k if up else k) + base, pl.ds(base, NHL)],
            dst_ref=fields[s].at[2 - k if up else NXL + 3 + k, pl.ds(3, NHL)],
            send_sem=sx.at[s, int(up), k],
            recv_sem=rx.at[s, int(up), k],
            device_id={"gx": (g + 1) % ng if up else (g + ng - 1) % ng, "head": hd},
            device_id_type=MESH,
        )

    def h_copy(s, up, chunk):
        src = level if s == 0 else fields[s]
        base = 0 if s == 0 else 3
        start = (NHL - 3 if up else 0) + base
        return pltpu.make_async_remote_copy(
            src_ref=src.at[pl.ds(3 * chunk + base, 3), pl.ds(start, 3)],
            dst_ref=fields[s].at[pl.ds(3 * chunk + 3, 3), pl.ds(0 if up else NHL + 3, 3)],
            send_sem=sh.at[s, int(up), chunk],
            recv_sem=rh.at[s, int(up), chunk],
            device_id={"gx": g, "head": (hd + 1) % nh if up else (hd + nh - 1) % nh},
            device_id_type=MESH,
        )

    def send_x(s, up):
        @pl.when(g < ng - 1 if up else g > 0)
        def _():
            for k in range(3):
                x_copy(s, up, k).start()

    def take_x(s, up):
        @pl.when(g > 0 if up else g < ng - 1)
        def _():
            for k in range(3):
                x_copy(s, up, k).wait_recv()

        @pl.when(g == 0 if up else g == ng - 1)
        def _():
            for h in range(NHL):
                edge = fields[s][3 if up else NXL + 2, h + 3]
                for i in range(3):
                    fields[s][i if up else NXL + 3 + i, h + 3] = edge

    def send_h(s, chunk):
        for up in (True, False):
            h_copy(s, up, chunk).start()

    def take_h(s, chunk):
        for up in (True, False):
            h_copy(s, up, chunk).wait_recv()

    to_root = lambda: pltpu.make_async_remote_copy(
        src_ref=pmine.at[0, pl.ds(0, 4)], dst_ref=pbuf.at[z, pl.ds(0, 4)], send_sem=sp.at[0], recv_sem=rp.at[z],
        device_id={"gx": at(yh, 0), "head": hd}, device_id_type=MESH,
    )
    to_other = lambda: pltpu.make_async_remote_copy(
        src_ref=pmine.at[0, pl.ds(0, 4)], dst_ref=pbuf.at[Z + z, pl.ds(0, 4)], send_sem=sp.at[1], recv_sem=rp.at[Z + z],
        device_id={"gx": at(1 - yh, 0), "head": across}, device_id_type=MESH,
    )
    answer = lambda i: pltpu.make_async_remote_copy(
        src_ref=pmine.at[1, pl.ds(0, 4)], dst_ref=pbuf.at[2 * Z, pl.ds(0, 4)], send_sem=sp.at[1 + i], recv_sem=rp.at[2 * Z],
        device_id={"gx": at(yh, i), "head": hd}, device_id_type=MESH,
    )
    arrived = lambda slot: pltpu.make_async_remote_copy(
        src_ref=pmine.at[0, pl.ds(0, 4)], dst_ref=pbuf.at[slot, pl.ds(0, 4)], send_sem=sp.at[0], recv_sem=rp.at[slot],
        device_id={"gx": at(1 - yh, 0), "head": across}, device_id_type=MESH,
    )

    greeters = 3 + (g > 0).astype(jnp.int32) + (g < ng - 1).astype(jnp.int32) + (z > 0).astype(jnp.int32)
    pl.semaphore_wait(barrier, greeters)

    @pl.when(z > 0)
    def _():
        to_root().start()

    to_other().start()
    send_x(0, True)
    send_x(0, False)
    for chunk in range(3):
        send_h(0, chunk)

    for i in range(NXL):
        wx[i] = jnp.broadcast_to(wv[i, 0:1, :], (NV, NY))
        wy[i] = jnp.broadcast_to(wv[i, 1:2, :], (NV, NY))
    get_mask.wait()
    get_depth.wait()
    for i in range(NXL):
        d = dv[i : i + 1, :]
        tg[i] = jnp.broadcast_to(jnp.where(mv[i : i + 1, :] == 1, -d, d), (NV, NY))
    get_tab.wait()
    get_level.wait()

    pass_vy(u0, rv, r, wx, wy, tab, bx, by, None)
    for chunk in range(3):
        take_h(0, chunk)
    def add(x, h, part):
        r[x, h] = (r[x, h] + rv[x, h]) + part

    pass_h(u0, 0, NXL, add)

    def keep(x, h, part, jump):
        r[x, h] = r[x, h] + part
        bx[x, h] = jump

    def either(low, first, second):
        pl.when(low)(first)
        pl.when(jnp.logical_not(low))(second)

    def both_sides(s, finish, after):
        turned = jnp.logical_or(g == Z, g == Z - 1)

        def body(j, carry):
            low = jnp.logical_xor(j == 0, turned)
            high = jnp.logical_not(low)
            seam = jnp.logical_and(s > 0, jnp.logical_and(turned, low == (g == Z)))
            plain = jnp.logical_not(seam)
            pl.when(jnp.logical_and(plain, low))(lambda: take_x(s, True))
            pl.when(jnp.logical_and(plain, high))(lambda: take_x(s, False))

            @pl.when(plain)
            def _():
                pass_x(fields[s], wx, tab, jnp.where(low, 0, 6), 3, 4, finish)

            if s == 1:
                pl.when(jnp.logical_and(plain, low))(lambda: send_x(2, False))
                pl.when(jnp.logical_and(plain, high))(lambda: send_x(2, True))
            if s > 0:

                @pl.when(seam)
                def _():
                    for k in range(3):
                        either(low, lambda: x_copy(s, True, k).wait_recv(), lambda: x_copy(s, False, k).wait_recv())
                        pass_x(fields[s], wx, tab, jnp.where(low, 2 - k, 6 + k), 1, NHL, finish)
                        if s == 1:
                            either(low, lambda: x_copy(2, False, 2 - k).start(), lambda: x_copy(2, True, 2 - k).start())

            either(low, lambda: after(0), lambda: after(2))
            return carry

        lax.fori_loop(0, 2, body, 0)

    both_sides(0, keep, lambda chunk: None)

    @pl.when(z == 0)
    def _():
        best = pmine[0, 0:4]
        for slot in range(1, 2 * Z):
            arrived(slot).wait_recv()
            best = jnp.maximum(best, pbuf[slot, 0:4])
        pmine[1, 0:4] = best
        for i in range(1, Z):
            answer(i).start()

    @pl.when(z > 0)
    def _():
        arrived(2 * Z).wait_recv()
        pmine[1, 0:4] = pbuf[2 * Z, 0:4]

    top = pmine[1, 0:4]
    cx, cnx, cy, cny = bounds()
    peak_x = jnp.maximum(top[0:1] + cx, top[1:2] + cnx)
    peak_y = jnp.maximum(top[2:3] + cy, top[3:4] + cny)
    step = courant / (peak_x / spacing + peak_y / spacing + turn_limit / HT + thrust_limit / HV)
    pk[0] = jnp.broadcast_to(peak_x, (NV, NY))
    pk[1] = jnp.broadcast_to(peak_y, (NV, NY))
    pk[2] = jnp.broadcast_to(step * (1.0 / (12.0 * spacing)), (NV, NY))

    def update_one(lo):
        def body(h, carry):
            px, py, dt = pk[0], pk[1], pk[2]
            for i in range(3):
                rate = r[lo + i, h] + px * bx[lo + i, h] + py * by[lo + i, h]
                u1[lo + i + 3, h + 3] = jnp.minimum(u0[lo + i + 3, h + 3] + dt * rate, tg[lo + i])
            return carry

        lax.fori_loop(0, NHL, body, 0, unroll=2)

    update_one(0)
    send_x(1, False)
    send_h(1, 0)
    update_one(6)
    send_x(1, True)
    send_h(1, 2)
    update_one(3)
    send_h(1, 1)

    def section(s, write, after):
        u = fields[s]
        old, new = (0.75, 0.25) if s == 1 else (1.0 / 3.0, 2.0 / 3.0)
        pass_vy(u, rv, r, wx, wy, tab, None, None, pk)

        def close(x, h, rate):
            now = old * u0[x + 3, h + 3] + new * (u[x + 3, h + 3] + pk[2] * rate)
            write(x, h, jnp.minimum(now, tg[x]))

        def finish_x(x, h, part, jump):
            close(x, h, (r[x, h] + part) + pk[0] * jump)

        def finish_h(x, h, part):
            close(x, h, (r[x, h] + rv[x, h]) + part)

        def middle():
            take_h(s, 1)
            pass_h(u, 3, 6, finish_h)
            after(1)

        for chunk in (0, 2):
            take_h(s, chunk)
            pass_h(u, 3 * chunk, 3 * chunk + 3, add)
        if s == 2:
            middle()
        else:
            pl.when(g == Z)(middle)
        both_sides(s, finish_x, after)
        if s == 1:
            pl.when(g != Z)(middle)

    def write_two(x, h, value):
        u2[x + 3, h + 3] = value

    section(1, write_two, lambda chunk: send_h(2, chunk))

    def write_out(x, h, value):
        out[x, h] = value

    section(2, write_out, lambda chunk: None)


    @pl.when(z > 0)
    def _():
        to_root().wait_send()

    to_other().wait_send()

    @pl.when(z == 0)
    def _():
        for i in range(1, Z):
            answer(i).wait_send()

    for s in range(3):
        for up in (True, False):

            @pl.when(g < ng - 1 if up else g > 0)
            def _():
                for k in range(3):
                    x_copy(s, up, k).wait_send()

            for chunk in range(3):
                h_copy(s, up, chunk).wait_send()


def local(level_set, wind_field, target_mask, target_depth):
    field = pltpu.VMEM((NXL + 6, NHL + 6, NV, NY), jnp.float32)
    inner = pltpu.VMEM((NXL, NHL, NV, NY), jnp.float32)
    rows = pltpu.VMEM((NXL, NV, NY), jnp.float32)
    dma = pltpu.SemaphoreType.DMA
    inputs = (level_set, jnp.transpose(wind_field, (1, 0, 2)), target_mask, target_depth, jnp.asarray(table()))
    return pl.pallas_call(
        kernel,
        out_shape=jax.ShapeDtypeStruct(level_set.shape, jnp.float32),
        in_specs=[pl.BlockSpec(memory_space=pltpu.HBM)] * 5,
        out_specs=pl.BlockSpec(memory_space=pltpu.VMEM),
        scratch_shapes=[
            field, field, field, inner, inner, inner, inner,
            pltpu.VMEM((NXL, 2, NY), jnp.float32),
            pltpu.VMEM((NXL, NY), jnp.int32),
            pltpu.VMEM((NXL, NY), jnp.float32),
            pltpu.VMEM((2 * NHL, NY), jnp.float32),
            rows, rows, rows,
            pltpu.VMEM((3, NV, NY), jnp.float32),
            pltpu.VMEM((2 * Z + 1, NV, NY), jnp.float32),
            pltpu.VMEM((2, NV, NY), jnp.float32),
            dma((5,)), dma((3, 2, 3)), dma((3, 2, 3)), dma((3, 2, 3)), dma((3, 2, 3)), dma((Z + 1,)), dma((2 * Z + 1,)),
        ],
        compiler_params=pltpu.CompilerParams(collective_id=0, has_side_effects=True, vmem_limit_bytes=32 * 1024 * 1024),
        name="step",
    )(*[pltpu.with_memory_space_constraint(a, pltpu.HBM) for a in inputs])


def solution(mesh):
    return jax.shard_map(
        local,
        mesh=mesh,
        in_specs=(P("gx", "head", None, None), P(None, "gx", None), P("gx", None), P("gx", None)),
        out_specs=P("gx", "head", None, None),
        check_vma=False,
    )
```

```python
import functools
import math

import jax
import jax.numpy as jnp
import numpy as np
from jax import lax
from jax.experimental import pallas as pl
from jax.experimental.pallas import tpu as pltpu
from jax.sharding import PartitionSpec as P

MESH = pl.DeviceIdType.MESH
epsilon = 1e-06
courant = 0.5
spacing = 0.05
turn_limit = 1.0
thrust_limit = 0.5
speed_low = 0.5
speed_high = 1.5
NV = 8
NY = 128
NX = 288
NTH = 192
NXL = 9
NHL = 12
HT = 2.0 * math.pi / NTH
HV = (speed_high - speed_low) / (NV - 1)
EPS_X = 0.75 * epsilon * spacing**2
EPS_T = 0.75 * epsilon * HT**2
EPS_V = 0.75 * epsilon * HV**2
K_T = turn_limit * spacing / HT
K_V = thrust_limit * spacing / HV
Z = 16


def face(p, q, hp, hq, eps, left, mid, right):
    b = q - p
    b2 = b + b
    smooth = (b * b + eps) + hp * q
    out = {"b2": b2}
    if left:
        s = smooth + hq * b2
        out["L"] = 1.0 / (s * s)
        out["aL"] = out["L"] * (1.0 / 3.0)
    if mid:
        out["M"] = 2.0 / (smooth * smooth)
    if right:
        s = smooth - hp * b2
        out["R"] = 1.0 / (s * s)
        out["aR"] = out["R"] * (1.0 / 3.0)
    return out


def join(a_lo, m_lo, c_lo, k_lo, a_hi, m_hi, c_hi, k_hi, c):
    low = (a_lo * k_lo + c_lo * c) / ((a_lo + c_lo) + m_lo)
    high = (a_hi * k_hi + c_hi * c) / ((a_hi + c_hi) + m_hi)
    return high - low, (high + low) - c


def line(load, n, eps):
    u = {i: load(i) for i in range(-3, n + 3)}
    d = {i: u[i + 1] - u[i] for i in range(-3, n + 2)}
    e = {i: d[i] - d[i - 1] for i in range(-2, n + 2)}
    h = {i: 0.75 * e[i] for i in e}
    f = {
        i: face(e[i], e[i + 1], h[i], h[i + 1], eps, i <= n - 2, -1 <= i <= n - 1, i >= 0)
        for i in range(-2, n + 1)
    }
    k = {i: f[i]["b2"] - f[i - 1]["b2"] for i in range(-1, n + 1)}
    g = {i: 6.0 * u[i] - e[i] for i in range(-1, n + 1)}
    return finished(f, k, g, n)


def along(u, axis, eps, first, last):
    n = u.shape[axis]
    back = lambda a: pltpu.roll(a, 1, axis)
    ahead = lambda a: pltpu.roll(a, n - 1, axis)
    d_lo = u - jnp.where(first, u, back(u))
    d_hi = jnp.where(last, u, ahead(u)) - u
    e = d_hi - d_lo
    p, q = jnp.where(first, 0.0, back(e)), jnp.where(last, 0.0, ahead(e))
    b_lo, b_hi = e - p, q - e
    h = 0.75 * e
    m_lo = (b_lo * b_lo + eps) + h * p
    m_hi = (b_hi * b_hi + eps) + h * q
    h2 = h + h
    s_lo = m_lo + h2 * b_lo
    s_hi = m_hi - h2 * b_hi
    c_hi = 1.0 / (s_lo * s_lo)
    c_lo = 1.0 / (s_hi * s_hi)
    c = b_hi - b_lo
    k = c + c
    e2 = e + e
    flat = 1.0 / (3.0 * eps * eps)
    a_lo = jnp.where(first, flat, back(c_hi * (1.0 / 3.0)))
    a_hi = jnp.where(last, flat, ahead(c_lo * (1.0 / 3.0)))
    k_lo = jnp.where(first, e2, back(k))
    k_hi = jnp.where(last, e2, ahead(k))
    diff, jump = join(a_lo, 2.0 / (m_lo * m_lo), c_lo, k_lo, a_hi, 2.0 / (m_hi * m_hi), c_hi, k_hi, c)
    return (6.0 * (d_hi + d_lo) - (q - p)) + diff, jump


def closed(load, n, eps):
    u = [load(i) for i in range(n)]
    d = [u[i + 1] - u[i] for i in range(n - 1)]
    e = [d[0]] + [d[i] - d[i - 1] for i in range(1, n - 1)] + [-d[n - 2]]
    h = [0.75 * a for a in e]
    f = {i: face(e[i], e[i + 1], h[i], h[i + 1], eps, True, True, True) for i in range(n - 1)}
    twice = [e[0] + e[0], e[n - 1] + e[n - 1]]
    rim = [e[0] * e[0] + eps, e[n - 1] * e[n - 1] + eps]
    out_l, out_r = rim[0] + h[0] * twice[0], rim[1] + h[n - 1] * twice[1]
    left, right = 1.0 / (out_l * out_l), 1.0 / (out_r * out_r)
    flat = 1.0 / (3.0 * eps * eps)
    f[-2], f[n] = {"aL": flat}, {"aR": flat}
    f[-1] = {"b2": twice[0], "L": left, "aL": left * (1.0 / 3.0), "M": 2.0 / (rim[0] * rim[0])}
    f[n - 1] = {"b2": -twice[1], "R": right, "aR": right * (1.0 / 3.0), "M": 2.0 / (rim[1] * rim[1])}
    k = {i: f[i]["b2"] - f[i - 1]["b2"] for i in range(n)}
    k[-1], k[n] = twice
    u6 = [6.0 * a for a in u]
    g = {i: u6[i] - e[i] for i in range(n)}
    g[-1], g[n] = u6[0], u6[n - 1]
    return finished(f, k, g, n)


def finished(f, k, g, n):
    result = []
    for i in range(n):
        diff, jump = join(
            f[i - 2]["aL"], f[i - 1]["M"], f[i]["R"], k[i - 1],
            f[i + 1]["aR"], f[i]["M"], f[i - 1]["L"], k[i + 1],
            0.5 * k[i],
        )
        result.append(((g[i + 1] - g[i - 1]) + diff, jump))
    return result


def iotas():
    shape = (NV, NY)
    row = lax.broadcasted_iota(jnp.int32, shape, 0)
    lane = lax.broadcasted_iota(jnp.int32, shape, 1)
    return row, lane


def speeds_of(row):
    return speed_low + row.astype(jnp.float32) * np.float32(HV)


def pass_vy(u_ref, v_ref, r_ref, wx_ref, wy_ref, tab_ref, bx_ref, by_ref, pk_ref):
    wide = NHL + 6
    u_rows = u_ref.reshape((NXL + 6) * wide * NV, NY)
    r_rows = v_ref.reshape(NXL * NHL * NV, NY)

    def speed_terms(x, h, along_x):
        u_at = ((x + 3) * wide + h + 3) * NV
        r_at = (x * NHL + h) * NV
        u_step, r_step = (wide * NV, NHL * NV) if along_x else (NV, NV)
        cells = closed(lambda v: u_rows[pl.ds(u_at + v, 8, stride=u_step), :], NV, EPS_V)
        for v, (total, jump) in enumerate(cells):
            r_rows[pl.ds(r_at + v, 8, stride=r_step), :] = K_V * (jump - jnp.abs(total))

    def y_terms(cells, extra={}):
        row, lane = iotas()
        speeds = speeds_of(row)
        y0, y1 = lane == 0, lane == NY - 1
        for x, h in cells:
            total, jump = along(u_ref[x + 3, h + 3], 1, EPS_X, y0, y1)
            rate = total * (speeds * tab_ref[pl.ds(NHL + h, 1), :] + wy_ref[x])
            if x in extra:
                rate = rate + extra[x]
            if by_ref is not None:
                by_ref[x, h] = jump
            else:
                rate = rate + pk_ref[1] * jump
            r_ref[x, h] = rate

    def middle_terms(h):
        row, _ = iotas()
        lanes = speeds_of(row) * tab_ref[pl.ds(h, 1), :]
        parts = {}
        for i, (total, jump) in enumerate(line(lambda i: u_ref[i + 6, h + 3], 3, EPS_X)):
            parts[3 + i] = total * (lanes + wx_ref[3 + i])
            if bx_ref is not None:
                bx_ref[3 + i, h] = jump
            else:
                parts[3 + i] = parts[3 + i] + pk_ref[0] * jump
        return parts

    def body(t, carry):
        for j in range(3):
            h = 3 * t + j
            parts = middle_terms(h)
            speed_terms(0, h, True)
            y_terms([(x, h) for x in range(8)], parts)
        return carry

    lax.fori_loop(0, NHL // 3, body, 0)
    for x in range(8, NXL):
        for h in (0, NHL - 8):
            speed_terms(x, h, False)
        y_terms([(x, h) for h in range(NHL)])


def pass_h(u_ref, lo, hi, finish):
    def plane(x):
        for h, (total, jump) in enumerate(line(lambda i: u_ref[x + 3, i + 3], NHL, EPS_T)):
            finish(x, h, K_T * (jump - jnp.abs(total)))

    def body(t, carry):
        for j in range(3):
            plane(lo + 3 * t + j)
        return carry

    if hi - lo == 3:
        body(0, 0)
    else:
        lax.fori_loop(0, (hi - lo) // 3, body, 0)


def pass_x(u_ref, wx_ref, tab_ref, lo, planes, group, finish):
    def body(t, carry):
        row, _ = iotas()
        speeds = speeds_of(row)
        for j in range(group):
            h = t * group + j
            lanes = speeds * tab_ref[pl.ds(h, 1), :]
            cells = line(lambda i: u_ref[lo + i + 3, h + 3], planes, EPS_X)
            for i, (total, jump) in enumerate(cells):
                finish(lo + i, h, total * (lanes + wx_ref[lo + i]), jump)
        return carry

    if group == NHL:
        body(0, 0)
    else:
        lax.fori_loop(0, NHL // group, body, 0)


def bounds():
    speeds = np.float32(speed_low) + np.arange(NV, dtype=np.float32) * np.float32(HV)
    angles = np.arange(NTH, dtype=np.float32) * np.float32(HT)
    px = np.cos(angles)[:, None] * speeds
    py = np.sin(angles)[:, None] * speeds
    return [float(a) for a in (px.max(), -px.min(), py.max(), -py.min())]


def table():
    angles = np.arange(NTH, dtype=np.float32) * np.float32(HT)
    both = np.stack([np.cos(angles).reshape(-1, NHL), np.sin(angles).reshape(-1, NHL)], 1)
    both = both.reshape(NTH // NHL, 2 * NHL, 1).astype(np.float32)
    return np.broadcast_to(both, (NTH // NHL, 2 * NHL, NY)).copy()


def kernel(
    level, wind, mask, depth, tab_all, out,
    u0, u1, u2, r, rv, bx, by, wv, mv, dv, tab, wx, wy, tg, pk, pbuf, pmine,
    sem_in, sx, rx, sh, rh, sp, rp,
):
    g = lax.axis_index("gx")
    hd = lax.axis_index("head")
    ng, nh = lax.axis_size("gx"), lax.axis_size("head")
    yh, z = g // Z, g % Z
    at = lambda half, z_: half * Z + z_
    across = (hd + nh // 2) % nh
    slow = (hd % 8 == 0).astype(jnp.int32)
    helper = (hd % 8 == 1).astype(jnp.int32)
    fields = (u0, u1, u2)

    get_wind = pltpu.make_async_copy(wind, wv, sem_in.at[0])
    get_wind.start()

    barrier = pltpu.get_barrier_semaphore()

    def greet(peer):
        pl.semaphore_signal(barrier, inc=1, device_id=peer, device_id_type=MESH)

    greet({"gx": g, "head": (hd + 1) % nh})
    greet({"gx": g, "head": (hd + nh - 1) % nh})

    @pl.when(g < ng - 1)
    def _():
        greet({"gx": (g + 1) % ng, "head": hd})

    @pl.when(g > 0)
    def _():
        greet({"gx": (g + ng - 1) % ng, "head": hd})

    @pl.when(z == 0)
    def _():
        for i in range(1, Z):
            greet({"gx": at(yh, i), "head": hd + slow})
        for i in range(Z):
            greet({"gx": at(1 - yh, i), "head": across + slow})

    get_level = pltpu.make_async_copy(level, u0.at[pl.ds(3, NXL), pl.ds(3, NHL)], sem_in.at[1])
    get_level.start()
    get_tab = pltpu.make_async_copy(tab_all.at[hd], tab, sem_in.at[2])
    get_tab.start()
    get_mask = pltpu.make_async_copy(mask, mv, sem_in.at[3])
    get_mask.start()
    get_depth = pltpu.make_async_copy(depth, dv, sem_in.at[4])
    get_depth.start()

    get_wind.wait()
    tops = []
    for c in range(2):
        top, low = wv[0, c : c + 1, :], wv[0, c : c + 1, :]
        for i in range(1, NXL):
            top, low = jnp.maximum(top, wv[i, c : c + 1, :]), jnp.minimum(low, wv[i, c : c + 1, :])
        tops += [top, -low]
    row, _ = iotas()
    tile = jnp.broadcast_to(tops[0], (NV, NY))
    for i in range(1, 4):
        tile = jnp.where(row == i, jnp.broadcast_to(tops[i], (NV, NY)), tile)
    pmine[0] = jnp.broadcast_to(jnp.max(tile, axis=1, keepdims=True), (NV, NY))

    def x_copy(s, up, k):
        src = level if s == 0 else fields[s]
        base = 0 if s == 0 else 3
        return pltpu.make_async_remote_copy(
            src_ref=src.at[(NXL - 1 - k if up else k) + base, pl.ds(base, NHL)],
            dst_ref=fields[s].at[2 - k if up else NXL + 3 + k, pl.ds(3, NHL)],
            send_sem=sx.at[s, int(up), k],
            recv_sem=rx.at[s, int(up), k],
            device_id={"gx": (g + 1) % ng if up else (g + ng - 1) % ng, "head": hd},
            device_id_type=MESH,
        )

    def h_copy(s, up, chunk):
        src = level if s == 0 else fields[s]
        base = 0 if s == 0 else 3
        start = (NHL - 3 if up else 0) + base
        return pltpu.make_async_remote_copy(
            src_ref=src.at[pl.ds(3 * chunk + base, 3), pl.ds(start, 3)],
            dst_ref=fields[s].at[pl.ds(3 * chunk + 3, 3), pl.ds(0 if up else NHL + 3, 3)],
            send_sem=sh.at[s, int(up), chunk],
            recv_sem=rh.at[s, int(up), chunk],
            device_id={"gx": g, "head": (hd + 1) % nh if up else (hd + nh - 1) % nh},
            device_id_type=MESH,
        )

    def send_x(s, up):
        @pl.when(g < ng - 1 if up else g > 0)
        def _():
            for k in range(3):
                x_copy(s, up, k).start()

    def take_x(s, up):
        @pl.when(g > 0 if up else g < ng - 1)
        def _():
            for k in range(3):
                x_copy(s, up, k).wait_recv()

        @pl.when(g == 0 if up else g == ng - 1)
        def _():
            for h in range(NHL):
                edge = fields[s][3 if up else NXL + 2, h + 3]
                for i in range(3):
                    fields[s][i if up else NXL + 3 + i, h + 3] = edge

    def send_h(s, chunk):
        for up in (True, False):
            h_copy(s, up, chunk).start()

    def take_h(s, chunk):
        for up in (True, False):
            h_copy(s, up, chunk).wait_recv()

    to_root = lambda back: pltpu.make_async_remote_copy(
        src_ref=pmine.at[0, pl.ds(0, 4)], dst_ref=pbuf.at[z, pl.ds(0, 4)], send_sem=sp.at[(Z + 1) * back], recv_sem=rp.at[z],
        device_id={"gx": at(yh, 0), "head": hd - back}, device_id_type=MESH,
    )
    to_other = lambda back: pltpu.make_async_remote_copy(
        src_ref=pmine.at[0, pl.ds(0, 4)], dst_ref=pbuf.at[Z + z, pl.ds(0, 4)], send_sem=sp.at[1 + (Z + 1) * back],
        recv_sem=rp.at[Z + z], device_id={"gx": at(1 - yh, 0), "head": across - back}, device_id_type=MESH,
    )

    def push(act):
        for back in (0, 1):
            who = helper == 1 if back else slow == 0

            @pl.when(jnp.logical_and(who, z > 0))
            def _():
                act(to_root(back))

            @pl.when(who)
            def _():
                act(to_other(back))

    answer = lambda i: pltpu.make_async_remote_copy(
        src_ref=pmine.at[1, pl.ds(0, 4)], dst_ref=pbuf.at[2 * Z, pl.ds(0, 4)], send_sem=sp.at[1 + i], recv_sem=rp.at[2 * Z],
        device_id={"gx": at(yh, i), "head": hd}, device_id_type=MESH,
    )
    arrived = lambda slot: pltpu.make_async_remote_copy(
        src_ref=pmine.at[0, pl.ds(0, 4)], dst_ref=pbuf.at[slot, pl.ds(0, 4)], send_sem=sp.at[0], recv_sem=rp.at[slot],
        device_id={"gx": at(1 - yh, 0), "head": across}, device_id_type=MESH,
    )

    roots = (1 + (z > 0).astype(jnp.int32)) * (1 + helper - slow)
    greeters = 2 + (g > 0).astype(jnp.int32) + (g < ng - 1).astype(jnp.int32) + roots
    pl.semaphore_wait(barrier, greeters)

    push(lambda copy: copy.start())
    send_x(0, True)
    send_x(0, False)
    for chunk in range(3):
        send_h(0, chunk)

    for i in range(NXL):
        wx[i] = jnp.broadcast_to(wv[i, 0:1, :], (NV, NY))
        wy[i] = jnp.broadcast_to(wv[i, 1:2, :], (NV, NY))
    get_mask.wait()
    get_depth.wait()
    for i in range(NXL):
        d = dv[i : i + 1, :]
        tg[i] = jnp.broadcast_to(jnp.where(mv[i : i + 1, :] == 1, -d, d), (NV, NY))
    get_tab.wait()
    get_level.wait()

    pass_vy(u0, rv, r, wx, wy, tab, bx, by, None)
    for chunk in range(3):
        take_h(0, chunk)
    def add(x, h, part):
        r[x, h] = (r[x, h] + rv[x, h]) + part

    pass_h(u0, 0, NXL, add)

    def keep(x, h, part, jump):
        r[x, h] = r[x, h] + part
        bx[x, h] = jump

    def either(low, first, second):
        pl.when(low)(first)
        pl.when(jnp.logical_not(low))(second)

    def both_sides(s, finish, after):
        turned = jnp.logical_or(g == Z, g == Z - 1)

        def body(j, carry):
            low = jnp.logical_xor(j == 0, turned)
            high = jnp.logical_not(low)
            seam = jnp.logical_and(s > 0, jnp.logical_and(turned, low == (g == Z)))
            plain = jnp.logical_not(seam)
            pl.when(jnp.logical_and(plain, low))(lambda: take_x(s, True))
            pl.when(jnp.logical_and(plain, high))(lambda: take_x(s, False))

            @pl.when(plain)
            def _():
                pass_x(fields[s], wx, tab, jnp.where(low, 0, 6), 3, NHL, finish)

            if s == 1:
                pl.when(jnp.logical_and(plain, low))(lambda: send_x(2, False))
                pl.when(jnp.logical_and(plain, high))(lambda: send_x(2, True))
            if s > 0:

                @pl.when(seam)
                def _():
                    for k in range(3):
                        either(low, lambda: x_copy(s, True, k).wait_recv(), lambda: x_copy(s, False, k).wait_recv())
                        pass_x(fields[s], wx, tab, jnp.where(low, 2 - k, 6 + k), 1, NHL, finish)
                        if s == 1:
                            either(low, lambda: x_copy(2, False, 2 - k).start(), lambda: x_copy(2, True, 2 - k).start())

            either(low, lambda: after(0), lambda: after(2))
            return carry

        lax.fori_loop(0, 2, body, 0)

    both_sides(0, keep, lambda chunk: None)

    @pl.when(z == 0)
    def _():
        best = pmine[0, 0:4]
        for slot in range(1, 2 * Z):
            arrived(slot).wait_recv()
            best = jnp.maximum(best, pbuf[slot, 0:4])
        pmine[1, 0:4] = best
        for i in range(1, Z):
            answer(i).start()

    @pl.when(z > 0)
    def _():
        arrived(2 * Z).wait_recv()
        pmine[1, 0:4] = pbuf[2 * Z, 0:4]

    top = pmine[1, 0:4]
    cx, cnx, cy, cny = bounds()
    peak_x = jnp.maximum(top[0:1] + cx, top[1:2] + cnx)
    peak_y = jnp.maximum(top[2:3] + cy, top[3:4] + cny)
    step = courant / (peak_x / spacing + peak_y / spacing + turn_limit / HT + thrust_limit / HV)
    pk[0] = jnp.broadcast_to(peak_x, (NV, NY))
    pk[1] = jnp.broadcast_to(peak_y, (NV, NY))
    pk[2] = jnp.broadcast_to(step * (1.0 / (12.0 * spacing)), (NV, NY))

    def update_one(lo):
        def body(h, carry):
            px, py, dt = pk[0], pk[1], pk[2]
            for i in range(3):
                rate = r[lo + i, h] + px * bx[lo + i, h] + py * by[lo + i, h]
                u1[lo + i + 3, h + 3] = jnp.minimum(u0[lo + i + 3, h + 3] + dt * rate, tg[lo + i])
            return carry

        lax.fori_loop(0, NHL, body, 0, unroll=2)

    update_one(0)
    send_x(1, False)
    send_h(1, 0)
    update_one(6)
    send_x(1, True)
    send_h(1, 2)
    update_one(3)
    send_h(1, 1)

    def section(s, write, after):
        u = fields[s]
        old, new = (0.75, 0.25) if s == 1 else (1.0 / 3.0, 2.0 / 3.0)
        pass_vy(u, rv, r, wx, wy, tab, None, None, pk)

        def close(x, h, rate):
            now = old * u0[x + 3, h + 3] + new * (u[x + 3, h + 3] + pk[2] * rate)
            write(x, h, jnp.minimum(now, tg[x]))

        def finish_x(x, h, part, jump):
            close(x, h, (r[x, h] + part) + pk[0] * jump)

        def finish_h(x, h, part):
            close(x, h, (r[x, h] + rv[x, h]) + part)

        def middle():
            take_h(s, 1)
            pass_h(u, 3, 6, finish_h)
            after(1)

        for chunk in (0, 2):
            take_h(s, chunk)
            pass_h(u, 3 * chunk, 3 * chunk + 3, add)
        if s == 2:
            middle()
        else:
            pl.when(g == Z)(middle)
        both_sides(s, finish_x, after)
        if s == 1:
            pl.when(g != Z)(middle)

    def write_two(x, h, value):
        u2[x + 3, h + 3] = value

    section(1, write_two, lambda chunk: send_h(2, chunk))

    def write_out(x, h, value):
        out[x, h] = value

    section(2, write_out, lambda chunk: None)


    push(lambda copy: copy.wait_send())

    @pl.when(z == 0)
    def _():
        for i in range(1, Z):
            answer(i).wait_send()

    for s in range(3):
        for up in (True, False):

            @pl.when(g < ng - 1 if up else g > 0)
            def _():
                for k in range(3):
                    x_copy(s, up, k).wait_send()

            for chunk in range(3):
                h_copy(s, up, chunk).wait_send()


def local(level_set, wind_field, target_mask, target_depth):
    field = pltpu.VMEM((NXL + 6, NHL + 6, NV, NY), jnp.float32)
    inner = pltpu.VMEM((NXL, NHL, NV, NY), jnp.float32)
    rows = pltpu.VMEM((NXL, NV, NY), jnp.float32)
    dma = pltpu.SemaphoreType.DMA
    inputs = (level_set, jnp.transpose(wind_field, (1, 0, 2)), target_mask, target_depth, jnp.asarray(table()))
    return pl.pallas_call(
        kernel,
        out_shape=jax.ShapeDtypeStruct(level_set.shape, jnp.float32),
        in_specs=[pl.BlockSpec(memory_space=pltpu.HBM)] * 5,
        out_specs=pl.BlockSpec(memory_space=pltpu.VMEM),
        scratch_shapes=[
            field, field, field, inner, inner, inner, inner,
            pltpu.VMEM((NXL, 2, NY), jnp.float32),
            pltpu.VMEM((NXL, NY), jnp.int32),
            pltpu.VMEM((NXL, NY), jnp.float32),
            pltpu.VMEM((2 * NHL, NY), jnp.float32),
            rows, rows, rows,
            pltpu.VMEM((3, NV, NY), jnp.float32),
            pltpu.VMEM((2 * Z + 1, NV, NY), jnp.float32),
            pltpu.VMEM((2, NV, NY), jnp.float32),
            dma((5,)), dma((3, 2, 3)), dma((3, 2, 3)), dma((3, 2, 3)), dma((3, 2, 3)), dma((Z + 3,)), dma((2 * Z + 1,)),
        ],
        compiler_params=pltpu.CompilerParams(collective_id=0, has_side_effects=True, vmem_limit_bytes=32 * 1024 * 1024),
        name="step",
    )(*[pltpu.with_memory_space_constraint(a, pltpu.HBM) for a in inputs])


def solution(mesh):
    return jax.shard_map(
        local,
        mesh=mesh,
        in_specs=(P("gx", "head", None, None), P(None, "gx", None), P("gx", None), P("gx", None)),
        out_specs=P("gx", "head", None, None),
        check_vma=False,
    )
```

```python
import functools
import math

import jax
import jax.numpy as jnp
import numpy as np
from jax import lax
from jax.experimental import pallas as pl
from jax.experimental.pallas import tpu as pltpu
from jax.sharding import PartitionSpec as P

MESH = pl.DeviceIdType.MESH
epsilon = 1e-06
courant = 0.5
spacing = 0.05
turn_limit = 1.0
thrust_limit = 0.5
speed_low = 0.5
speed_high = 1.5
NV = 8
NY = 128
NX = 288
NTH = 192
NXL = 9
NHL = 12
HT = 2.0 * math.pi / NTH
HV = (speed_high - speed_low) / (NV - 1)
EPS_X = 0.75 * epsilon * spacing**2
EPS_T = 0.75 * epsilon * HT**2
EPS_V = 0.75 * epsilon * HV**2
K_T = turn_limit * spacing / HT
K_V = thrust_limit * spacing / HV
Z = 16


def face(p, q, hp, hq, eps, left, mid, right):
    b = q - p
    b2 = b + b
    smooth = (b * b + eps) + hp * q
    out = {"b2": b2}
    if left:
        s = smooth + hq * b2
        out["L"] = 1.0 / (s * s)
        out["aL"] = out["L"] * (1.0 / 3.0)
    if mid:
        out["M"] = 2.0 / (smooth * smooth)
    if right:
        s = smooth - hp * b2
        out["R"] = 1.0 / (s * s)
        out["aR"] = out["R"] * (1.0 / 3.0)
    return out


def join(a_lo, m_lo, c_lo, k_lo, a_hi, m_hi, c_hi, k_hi, c):
    low = (a_lo * k_lo + c_lo * c) / ((a_lo + c_lo) + m_lo)
    high = (a_hi * k_hi + c_hi * c) / ((a_hi + c_hi) + m_hi)
    return high - low, (high + low) - c


def line(load, n, eps):
    u = {i: load(i) for i in range(-3, n + 3)}
    d = {i: u[i + 1] - u[i] for i in range(-3, n + 2)}
    e = {i: d[i] - d[i - 1] for i in range(-2, n + 2)}
    h = {i: 0.75 * e[i] for i in e}
    f = {
        i: face(e[i], e[i + 1], h[i], h[i + 1], eps, i <= n - 2, -1 <= i <= n - 1, i >= 0)
        for i in range(-2, n + 1)
    }
    k = {i: f[i]["b2"] - f[i - 1]["b2"] for i in range(-1, n + 1)}
    g = {i: 6.0 * u[i] - e[i] for i in range(-1, n + 1)}
    return finished(f, k, g, n)


def along(u, axis, eps, first, last):
    n = u.shape[axis]
    back = lambda a: pltpu.roll(a, 1, axis)
    ahead = lambda a: pltpu.roll(a, n - 1, axis)
    d_lo = u - jnp.where(first, u, back(u))
    d_hi = jnp.where(last, u, ahead(u)) - u
    e = d_hi - d_lo
    p, q = jnp.where(first, 0.0, back(e)), jnp.where(last, 0.0, ahead(e))
    b_lo, b_hi = e - p, q - e
    h = 0.75 * e
    m_lo = (b_lo * b_lo + eps) + h * p
    m_hi = (b_hi * b_hi + eps) + h * q
    h2 = h + h
    s_lo = m_lo + h2 * b_lo
    s_hi = m_hi - h2 * b_hi
    c_hi = 1.0 / (s_lo * s_lo)
    c_lo = 1.0 / (s_hi * s_hi)
    c = b_hi - b_lo
    k = c + c
    e2 = e + e
    flat = 1.0 / (3.0 * eps * eps)
    a_lo = jnp.where(first, flat, back(c_hi * (1.0 / 3.0)))
    a_hi = jnp.where(last, flat, ahead(c_lo * (1.0 / 3.0)))
    k_lo = jnp.where(first, e2, back(k))
    k_hi = jnp.where(last, e2, ahead(k))
    diff, jump = join(a_lo, 2.0 / (m_lo * m_lo), c_lo, k_lo, a_hi, 2.0 / (m_hi * m_hi), c_hi, k_hi, c)
    return (6.0 * (d_hi + d_lo) - (q - p)) + diff, jump


def closed(load, n, eps):
    u = [load(i) for i in range(n)]
    d = [u[i + 1] - u[i] for i in range(n - 1)]
    e = [d[0]] + [d[i] - d[i - 1] for i in range(1, n - 1)] + [-d[n - 2]]
    h = [0.75 * a for a in e]
    f = {i: face(e[i], e[i + 1], h[i], h[i + 1], eps, True, True, True) for i in range(n - 1)}
    twice = [e[0] + e[0], e[n - 1] + e[n - 1]]
    rim = [e[0] * e[0] + eps, e[n - 1] * e[n - 1] + eps]
    out_l, out_r = rim[0] + h[0] * twice[0], rim[1] + h[n - 1] * twice[1]
    left, right = 1.0 / (out_l * out_l), 1.0 / (out_r * out_r)
    flat = 1.0 / (3.0 * eps * eps)
    f[-2], f[n] = {"aL": flat}, {"aR": flat}
    f[-1] = {"b2": twice[0], "L": left, "aL": left * (1.0 / 3.0), "M": 2.0 / (rim[0] * rim[0])}
    f[n - 1] = {"b2": -twice[1], "R": right, "aR": right * (1.0 / 3.0), "M": 2.0 / (rim[1] * rim[1])}
    k = {i: f[i]["b2"] - f[i - 1]["b2"] for i in range(n)}
    k[-1], k[n] = twice
    u6 = [6.0 * a for a in u]
    g = {i: u6[i] - e[i] for i in range(n)}
    g[-1], g[n] = u6[0], u6[n - 1]
    return finished(f, k, g, n)


def finished(f, k, g, n):
    result = []
    for i in range(n):
        diff, jump = join(
            f[i - 2]["aL"], f[i - 1]["M"], f[i]["R"], k[i - 1],
            f[i + 1]["aR"], f[i]["M"], f[i - 1]["L"], k[i + 1],
            0.5 * k[i],
        )
        result.append(((g[i + 1] - g[i - 1]) + diff, jump))
    return result


def iotas():
    shape = (NV, NY)
    row = lax.broadcasted_iota(jnp.int32, shape, 0)
    lane = lax.broadcasted_iota(jnp.int32, shape, 1)
    return row, lane


def speeds_of(row):
    return speed_low + row.astype(jnp.float32) * np.float32(HV)


def pass_vy(u_ref, v_ref, r_ref, wx_ref, wy_ref, tab_ref, bx_ref, by_ref, pk_ref):
    wide = NHL + 6
    u_rows = u_ref.reshape((NXL + 6) * wide * NV, NY)
    r_rows = v_ref.reshape(NXL * NHL * NV, NY)

    def speed_terms(x, h, along_x):
        u_at = ((x + 3) * wide + h + 3) * NV
        r_at = (x * NHL + h) * NV
        u_step, r_step = (wide * NV, NHL * NV) if along_x else (NV, NV)
        cells = closed(lambda v: u_rows[pl.ds(u_at + v, 8, stride=u_step), :], NV, EPS_V)
        for v, (total, jump) in enumerate(cells):
            r_rows[pl.ds(r_at + v, 8, stride=r_step), :] = K_V * (jump - jnp.abs(total))

    def y_terms(cells, extra={}):
        row, lane = iotas()
        speeds = speeds_of(row)
        y0, y1 = lane == 0, lane == NY - 1
        for x, h in cells:
            total, jump = along(u_ref[x + 3, h + 3], 1, EPS_X, y0, y1)
            rate = total * (speeds * tab_ref[pl.ds(NHL + h, 1), :] + wy_ref[x])
            if x in extra:
                rate = rate + extra[x]
            if by_ref is not None:
                by_ref[x, h] = jump
            else:
                rate = rate + pk_ref[1] * jump
            r_ref[x, h] = rate

    def middle_terms(h):
        row, _ = iotas()
        lanes = speeds_of(row) * tab_ref[pl.ds(h, 1), :]
        parts = {}
        for i, (total, jump) in enumerate(line(lambda i: u_ref[i + 6, h + 3], 3, EPS_X)):
            parts[3 + i] = total * (lanes + wx_ref[3 + i])
            if bx_ref is not None:
                bx_ref[3 + i, h] = jump
            else:
                parts[3 + i] = parts[3 + i] + pk_ref[0] * jump
        return parts

    def body(t, carry):
        for j in range(3):
            h = 3 * t + j
            parts = middle_terms(h)
            speed_terms(0, h, True)
            y_terms([(x, h) for x in range(8)], parts)
        return carry

    lax.fori_loop(0, NHL // 3, body, 0)
    for x in range(8, NXL):
        for h in (0, NHL - 8):
            speed_terms(x, h, False)
        y_terms([(x, h) for h in range(NHL)])


def pass_h(u_ref, lo, planes, finish):
    def plane(x):
        for h, (total, jump) in enumerate(line(lambda i: u_ref[x + 3, i + 3], NHL, EPS_T)):
            finish(x, h, K_T * (jump - jnp.abs(total)))

    def body(t, carry):
        for j in range(3):
            plane(lo + 3 * t + j)
        return carry

    if planes == 3:
        body(0, 0)
    else:
        lax.fori_loop(0, planes // 3, body, 0)


def pass_x(u_ref, wx_ref, tab_ref, lo, planes, group, finish):
    def body(t, carry):
        row, _ = iotas()
        speeds = speeds_of(row)
        for j in range(group):
            h = t * group + j
            lanes = speeds * tab_ref[pl.ds(h, 1), :]
            cells = line(lambda i: u_ref[lo + i + 3, h + 3], planes, EPS_X)
            for i, (total, jump) in enumerate(cells):
                finish(lo + i, h, total * (lanes + wx_ref[lo + i]), jump)
        return carry

    if group == NHL:
        body(0, 0)
    else:
        lax.fori_loop(0, NHL // group, body, 0)


def bounds():
    speeds = np.float32(speed_low) + np.arange(NV, dtype=np.float32) * np.float32(HV)
    angles = np.arange(NTH, dtype=np.float32) * np.float32(HT)
    px = np.cos(angles)[:, None] * speeds
    py = np.sin(angles)[:, None] * speeds
    return [float(a) for a in (px.max(), -px.min(), py.max(), -py.min())]


def table():
    angles = np.arange(NTH, dtype=np.float32) * np.float32(HT)
    both = np.stack([np.cos(angles).reshape(-1, NHL), np.sin(angles).reshape(-1, NHL)], 1)
    both = both.reshape(NTH // NHL, 2 * NHL, 1).astype(np.float32)
    return np.broadcast_to(both, (NTH // NHL, 2 * NHL, NY)).copy()


def kernel(
    level, wind, mask, depth, tab_all, out,
    u0, u1, u2, r, rv, bx, by, wv, mv, dv, tab, wx, wy, tg, pk, pbuf, pmine,
    sem_in, sx, rx, sh, rh, sp, rp,
):
    g = lax.axis_index("gx")
    hd = lax.axis_index("head")
    ng, nh = lax.axis_size("gx"), lax.axis_size("head")
    yh, z = g // Z, g % Z
    at = lambda half, z_: half * Z + z_
    across = (hd + nh // 2) % nh
    slow = (hd % 8 == 0).astype(jnp.int32)
    helper = (hd % 8 == 1).astype(jnp.int32)
    fields = (u0, u1, u2)

    get_wind = pltpu.make_async_copy(wind, wv, sem_in.at[0])
    get_wind.start()

    barrier = pltpu.get_barrier_semaphore()

    def greet(peer):
        pl.semaphore_signal(barrier, inc=1, device_id=peer, device_id_type=MESH)

    greet({"gx": g, "head": (hd + 1) % nh})
    greet({"gx": g, "head": (hd + nh - 1) % nh})

    @pl.when(g < ng - 1)
    def _():
        greet({"gx": (g + 1) % ng, "head": hd})

    @pl.when(g > 0)
    def _():
        greet({"gx": (g + ng - 1) % ng, "head": hd})

    @pl.when(z == 0)
    def _():
        for i in range(1, Z):
            greet({"gx": at(yh, i), "head": hd + slow})
        for i in range(Z):
            greet({"gx": at(1 - yh, i), "head": across + slow})

    get_level = pltpu.make_async_copy(level, u0.at[pl.ds(3, NXL), pl.ds(3, NHL)], sem_in.at[1])
    get_level.start()
    get_tab = pltpu.make_async_copy(tab_all.at[hd], tab, sem_in.at[2])
    get_tab.start()
    get_mask = pltpu.make_async_copy(mask, mv, sem_in.at[3])
    get_mask.start()
    get_depth = pltpu.make_async_copy(depth, dv, sem_in.at[4])
    get_depth.start()

    get_wind.wait()
    tops = []
    for c in range(2):
        top, low = wv[0, c : c + 1, :], wv[0, c : c + 1, :]
        for i in range(1, NXL):
            top, low = jnp.maximum(top, wv[i, c : c + 1, :]), jnp.minimum(low, wv[i, c : c + 1, :])
        tops += [top, -low]
    row, _ = iotas()
    tile = jnp.broadcast_to(tops[0], (NV, NY))
    for i in range(1, 4):
        tile = jnp.where(row == i, jnp.broadcast_to(tops[i], (NV, NY)), tile)
    pmine[0] = jnp.broadcast_to(jnp.max(tile, axis=1, keepdims=True), (NV, NY))

    def x_copy(s, up, k):
        src = level if s == 0 else fields[s]
        base = 0 if s == 0 else 3
        return pltpu.make_async_remote_copy(
            src_ref=src.at[(NXL - 1 - k if up else k) + base, pl.ds(base, NHL)],
            dst_ref=fields[s].at[2 - k if up else NXL + 3 + k, pl.ds(3, NHL)],
            send_sem=sx.at[s, int(up), k],
            recv_sem=rx.at[s, int(up), k],
            device_id={"gx": (g + 1) % ng if up else (g + ng - 1) % ng, "head": hd},
            device_id_type=MESH,
        )

    def h_copy(s, up, chunk):
        src = level if s == 0 else fields[s]
        base = 0 if s == 0 else 3
        start = (NHL - 3 if up else 0) + base
        return pltpu.make_async_remote_copy(
            src_ref=src.at[pl.ds(3 * chunk + base, 3), pl.ds(start, 3)],
            dst_ref=fields[s].at[pl.ds(3 * chunk + 3, 3), pl.ds(0 if up else NHL + 3, 3)],
            send_sem=sh.at[s, int(up), chunk],
            recv_sem=rh.at[s, int(up), chunk],
            device_id={"gx": g, "head": (hd + 1) % nh if up else (hd + nh - 1) % nh},
            device_id_type=MESH,
        )

    def send_x(s, up):
        @pl.when(g < ng - 1 if up else g > 0)
        def _():
            for k in range(3):
                x_copy(s, up, k).start()

    def take_x(s, up):
        @pl.when(g > 0 if up else g < ng - 1)
        def _():
            for k in range(3):
                x_copy(s, up, k).wait_recv()

        @pl.when(g == 0 if up else g == ng - 1)
        def _():
            for h in range(NHL):
                edge = fields[s][3 if up else NXL + 2, h + 3]
                for i in range(3):
                    fields[s][i if up else NXL + 3 + i, h + 3] = edge

    def send_h(s, chunk):
        for up in (True, False):
            h_copy(s, up, chunk).start()

    def take_h(s, chunk):
        for up in (True, False):
            h_copy(s, up, chunk).wait_recv()

    to_root = lambda back: pltpu.make_async_remote_copy(
        src_ref=pmine.at[0, pl.ds(0, 4)], dst_ref=pbuf.at[z, pl.ds(0, 4)], send_sem=sp.at[(Z + 1) * back], recv_sem=rp.at[z],
        device_id={"gx": at(yh, 0), "head": hd - back}, device_id_type=MESH,
    )
    to_other = lambda back: pltpu.make_async_remote_copy(
        src_ref=pmine.at[0, pl.ds(0, 4)], dst_ref=pbuf.at[Z + z, pl.ds(0, 4)], send_sem=sp.at[1 + (Z + 1) * back],
        recv_sem=rp.at[Z + z], device_id={"gx": at(1 - yh, 0), "head": across - back}, device_id_type=MESH,
    )

    def push(act):
        for back in (0, 1):
            who = helper == 1 if back else slow == 0

            @pl.when(jnp.logical_and(who, z > 0))
            def _():
                act(to_root(back))

            @pl.when(who)
            def _():
                act(to_other(back))

    answer = lambda i: pltpu.make_async_remote_copy(
        src_ref=pmine.at[1, pl.ds(0, 4)], dst_ref=pbuf.at[2 * Z, pl.ds(0, 4)], send_sem=sp.at[1 + i], recv_sem=rp.at[2 * Z],
        device_id={"gx": at(yh, i), "head": hd}, device_id_type=MESH,
    )
    arrived = lambda slot: pltpu.make_async_remote_copy(
        src_ref=pmine.at[0, pl.ds(0, 4)], dst_ref=pbuf.at[slot, pl.ds(0, 4)], send_sem=sp.at[0], recv_sem=rp.at[slot],
        device_id={"gx": at(1 - yh, 0), "head": across}, device_id_type=MESH,
    )

    roots = (1 + (z > 0).astype(jnp.int32)) * (1 + helper - slow)
    greeters = 2 + (g > 0).astype(jnp.int32) + (g < ng - 1).astype(jnp.int32) + roots
    pl.semaphore_wait(barrier, greeters)

    push(lambda copy: copy.start())
    send_x(0, True)
    send_x(0, False)
    for chunk in range(3):
        send_h(0, chunk)

    for i in range(NXL):
        wx[i] = jnp.broadcast_to(wv[i, 0:1, :], (NV, NY))
        wy[i] = jnp.broadcast_to(wv[i, 1:2, :], (NV, NY))
    get_mask.wait()
    get_depth.wait()
    for i in range(NXL):
        d = dv[i : i + 1, :]
        tg[i] = jnp.broadcast_to(jnp.where(mv[i : i + 1, :] == 1, -d, d), (NV, NY))
    get_tab.wait()
    get_level.wait()

    pass_vy(u0, rv, r, wx, wy, tab, bx, by, None)
    for chunk in range(3):
        take_h(0, chunk)
    def add(x, h, part):
        r[x, h] = (r[x, h] + rv[x, h]) + part

    pass_h(u0, 0, NXL, add)

    def keep(x, h, part, jump):
        r[x, h] = r[x, h] + part
        bx[x, h] = jump

    def either(low, first, second):
        pl.when(low)(first)
        pl.when(jnp.logical_not(low))(second)

    def both_sides(s, finish, after):
        turned = jnp.logical_or(g == Z, g == Z - 1)

        def body(j, carry):
            low = jnp.logical_xor(j == 0, turned)
            high = jnp.logical_not(low)
            seam = jnp.logical_and(s > 0, jnp.logical_and(turned, low == (g == Z)))
            plain = jnp.logical_not(seam)
            if s > 0:
                either(low, lambda: take_h(s, 0), lambda: take_h(s, 2))
                pass_h(fields[s], jnp.where(low, 0, 6), 3, add)
            pl.when(jnp.logical_and(plain, low))(lambda: take_x(s, True))
            pl.when(jnp.logical_and(plain, high))(lambda: take_x(s, False))

            @pl.when(plain)
            def _():
                pass_x(fields[s], wx, tab, jnp.where(low, 0, 6), 3, NHL, finish)

            if s == 1:
                pl.when(jnp.logical_and(plain, low))(lambda: send_x(2, False))
                pl.when(jnp.logical_and(plain, high))(lambda: send_x(2, True))
            if s > 0:

                @pl.when(seam)
                def _():
                    for k in range(3):
                        either(low, lambda: x_copy(s, True, k).wait_recv(), lambda: x_copy(s, False, k).wait_recv())
                        pass_x(fields[s], wx, tab, jnp.where(low, 2 - k, 6 + k), 1, NHL, finish)
                        if s == 1:
                            either(low, lambda: x_copy(2, False, 2 - k).start(), lambda: x_copy(2, True, 2 - k).start())

            either(low, lambda: after(0), lambda: after(2))
            return carry

        lax.fori_loop(0, 2, body, 0)

    both_sides(0, keep, lambda chunk: None)

    @pl.when(z == 0)
    def _():
        best = pmine[0, 0:4]
        for slot in range(1, 2 * Z):
            arrived(slot).wait_recv()
            best = jnp.maximum(best, pbuf[slot, 0:4])
        pmine[1, 0:4] = best
        for i in (Z - 1, *range(1, Z - 1)):
            answer(i).start()

    @pl.when(z > 0)
    def _():
        arrived(2 * Z).wait_recv()
        pmine[1, 0:4] = pbuf[2 * Z, 0:4]

    top = pmine[1, 0:4]
    cx, cnx, cy, cny = bounds()
    peak_x = jnp.maximum(top[0:1] + cx, top[1:2] + cnx)
    peak_y = jnp.maximum(top[2:3] + cy, top[3:4] + cny)
    step = courant / (peak_x / spacing + peak_y / spacing + turn_limit / HT + thrust_limit / HV)
    pk[0] = jnp.broadcast_to(peak_x, (NV, NY))
    pk[1] = jnp.broadcast_to(peak_y, (NV, NY))
    pk[2] = jnp.broadcast_to(step * (1.0 / (12.0 * spacing)), (NV, NY))

    def update_one(lo):
        def body(h, carry):
            px, py, dt = pk[0], pk[1], pk[2]
            for i in range(3):
                rate = r[lo + i, h] + px * bx[lo + i, h] + py * by[lo + i, h]
                u1[lo + i + 3, h + 3] = jnp.minimum(u0[lo + i + 3, h + 3] + dt * rate, tg[lo + i])
            return carry

        lax.fori_loop(0, NHL, body, 0, unroll=2)

    update_one(0)
    send_x(1, False)
    send_h(1, 0)
    update_one(6)
    send_x(1, True)
    send_h(1, 2)
    update_one(3)
    send_h(1, 1)

    def section(s, write, after):
        u = fields[s]
        old, new = (0.75, 0.25) if s == 1 else (1.0 / 3.0, 2.0 / 3.0)
        pass_vy(u, rv, r, wx, wy, tab, None, None, pk)

        def close(x, h, rate):
            now = old * u0[x + 3, h + 3] + new * (u[x + 3, h + 3] + pk[2] * rate)
            write(x, h, jnp.minimum(now, tg[x]))

        def finish_x(x, h, part, jump):
            close(x, h, (r[x, h] + part) + pk[0] * jump)

        def finish_h(x, h, part):
            close(x, h, (r[x, h] + rv[x, h]) + part)

        def middle():
            take_h(s, 1)
            pass_h(u, 3, 3, finish_h)
            after(1)

        if s == 2:
            middle()
        else:
            pl.when(g == Z)(middle)
        both_sides(s, finish_x, after)
        if s == 1:
            pl.when(g != Z)(middle)

    def write_two(x, h, value):
        u2[x + 3, h + 3] = value

    section(1, write_two, lambda chunk: send_h(2, chunk))

    def write_out(x, h, value):
        out[x, h] = value

    section(2, write_out, lambda chunk: None)


    push(lambda copy: copy.wait_send())

    @pl.when(z == 0)
    def _():
        for i in range(1, Z):
            answer(i).wait_send()

    for s in range(3):
        for up in (True, False):

            @pl.when(g < ng - 1 if up else g > 0)
            def _():
                for k in range(3):
                    x_copy(s, up, k).wait_send()

            for chunk in range(3):
                h_copy(s, up, chunk).wait_send()


def local(level_set, wind_field, target_mask, target_depth):
    field = pltpu.VMEM((NXL + 6, NHL + 6, NV, NY), jnp.float32)
    inner = pltpu.VMEM((NXL, NHL, NV, NY), jnp.float32)
    rows = pltpu.VMEM((NXL, NV, NY), jnp.float32)
    dma = pltpu.SemaphoreType.DMA
    inputs = (level_set, jnp.transpose(wind_field, (1, 0, 2)), target_mask, target_depth, jnp.asarray(table()))
    return pl.pallas_call(
        kernel,
        out_shape=jax.ShapeDtypeStruct(level_set.shape, jnp.float32),
        in_specs=[pl.BlockSpec(memory_space=pltpu.HBM)] * 5,
        out_specs=pl.BlockSpec(memory_space=pltpu.VMEM),
        scratch_shapes=[
            field, field, field, inner, inner, inner, inner,
            pltpu.VMEM((NXL, 2, NY), jnp.float32),
            pltpu.VMEM((NXL, NY), jnp.int32),
            pltpu.VMEM((NXL, NY), jnp.float32),
            pltpu.VMEM((2 * NHL, NY), jnp.float32),
            rows, rows, rows,
            pltpu.VMEM((3, NV, NY), jnp.float32),
            pltpu.VMEM((2 * Z + 1, NV, NY), jnp.float32),
            pltpu.VMEM((2, NV, NY), jnp.float32),
            dma((5,)), dma((3, 2, 3)), dma((3, 2, 3)), dma((3, 2, 3)), dma((3, 2, 3)), dma((Z + 3,)), dma((2 * Z + 1,)),
        ],
        compiler_params=pltpu.CompilerParams(collective_id=0, has_side_effects=True, vmem_limit_bytes=32 * 1024 * 1024),
        name="step",
    )(*[pltpu.with_memory_space_constraint(a, pltpu.HBM) for a in inputs])


def solution(mesh):
    return jax.shard_map(
        local,
        mesh=mesh,
        in_specs=(P("gx", "head", None, None), P(None, "gx", None), P("gx", None), P("gx", None)),
        out_specs=P("gx", "head", None, None),
        check_vma=False,
    )
```

```python
import functools
import math

import jax
import jax.numpy as jnp
import numpy as np
from jax import lax
from jax.experimental import pallas as pl
from jax.experimental.pallas import tpu as pltpu
from jax.sharding import PartitionSpec as P

MESH = pl.DeviceIdType.MESH
epsilon = 1e-06
courant = 0.5
spacing = 0.05
turn_limit = 1.0
thrust_limit = 0.5
speed_low = 0.5
speed_high = 1.5
NV = 8
NY = 128
NX = 288
NTH = 192
NXL = 9
NHL = 12
HT = 2.0 * math.pi / NTH
HV = (speed_high - speed_low) / (NV - 1)
EPS_X = 0.75 * epsilon * spacing**2
EPS_T = 0.75 * epsilon * HT**2
EPS_V = 0.75 * epsilon * HV**2
K_T = turn_limit * spacing / HT
K_V = thrust_limit * spacing / HV
Z = 16


def face(p, q, hp, hq, eps, left, mid, right):
    b = q - p
    b2 = b + b
    smooth = (b * b + eps) + hp * q
    out = {"b2": b2}
    if left:
        s = smooth + hq * b2
        out["L"] = 1.0 / (s * s)
        out["aL"] = out["L"] * (1.0 / 3.0)
    if mid:
        out["M"] = 2.0 / (smooth * smooth)
    if right:
        s = smooth - hp * b2
        out["R"] = 1.0 / (s * s)
        out["aR"] = out["R"] * (1.0 / 3.0)
    return out


def join(a_lo, m_lo, c_lo, k_lo, a_hi, m_hi, c_hi, k_hi, c):
    low = (a_lo * k_lo + c_lo * c) / ((a_lo + c_lo) + m_lo)
    high = (a_hi * k_hi + c_hi * c) / ((a_hi + c_hi) + m_hi)
    return high - low, (high + low) - c


def line(load, n, eps):
    u = {i: load(i) for i in range(-3, n + 3)}
    d = {i: u[i + 1] - u[i] for i in range(-3, n + 2)}
    e = {i: d[i] - d[i - 1] for i in range(-2, n + 2)}
    h = {i: 0.75 * e[i] for i in e}
    f = {
        i: face(e[i], e[i + 1], h[i], h[i + 1], eps, i <= n - 2, -1 <= i <= n - 1, i >= 0)
        for i in range(-2, n + 1)
    }
    k = {i: f[i]["b2"] - f[i - 1]["b2"] for i in range(-1, n + 1)}
    g = {i: 6.0 * u[i] - e[i] for i in range(-1, n + 1)}
    return finished(f, k, g, n)


def along(u, axis, eps, first, last):
    n = u.shape[axis]
    back = lambda a: pltpu.roll(a, 1, axis)
    ahead = lambda a: pltpu.roll(a, n - 1, axis)
    d_lo = u - jnp.where(first, u, back(u))
    d_hi = jnp.where(last, u, ahead(u)) - u
    e = d_hi - d_lo
    p, q = jnp.where(first, 0.0, back(e)), jnp.where(last, 0.0, ahead(e))
    b_lo, b_hi = e - p, q - e
    h = 0.75 * e
    m_lo = (b_lo * b_lo + eps) + h * p
    m_hi = (b_hi * b_hi + eps) + h * q
    h2 = h + h
    s_lo = m_lo + h2 * b_lo
    s_hi = m_hi - h2 * b_hi
    c_hi = 1.0 / (s_lo * s_lo)
    c_lo = 1.0 / (s_hi * s_hi)
    c = b_hi - b_lo
    k = c + c
    e2 = e + e
    flat = 1.0 / (3.0 * eps * eps)
    a_lo = jnp.where(first, flat, back(c_hi * (1.0 / 3.0)))
    a_hi = jnp.where(last, flat, ahead(c_lo * (1.0 / 3.0)))
    k_lo = jnp.where(first, e2, back(k))
    k_hi = jnp.where(last, e2, ahead(k))
    diff, jump = join(a_lo, 2.0 / (m_lo * m_lo), c_lo, k_lo, a_hi, 2.0 / (m_hi * m_hi), c_hi, k_hi, c)
    return (6.0 * (d_hi + d_lo) - (q - p)) + diff, jump


def closed(load, n, eps):
    u = [load(i) for i in range(n)]
    d = [u[i + 1] - u[i] for i in range(n - 1)]
    e = [d[0]] + [d[i] - d[i - 1] for i in range(1, n - 1)] + [-d[n - 2]]
    h = [0.75 * a for a in e]
    f = {i: face(e[i], e[i + 1], h[i], h[i + 1], eps, True, True, True) for i in range(n - 1)}
    twice = [e[0] + e[0], e[n - 1] + e[n - 1]]
    rim = [e[0] * e[0] + eps, e[n - 1] * e[n - 1] + eps]
    out_l, out_r = rim[0] + h[0] * twice[0], rim[1] + h[n - 1] * twice[1]
    left, right = 1.0 / (out_l * out_l), 1.0 / (out_r * out_r)
    flat = 1.0 / (3.0 * eps * eps)
    f[-2], f[n] = {"aL": flat}, {"aR": flat}
    f[-1] = {"b2": twice[0], "L": left, "aL": left * (1.0 / 3.0), "M": 2.0 / (rim[0] * rim[0])}
    f[n - 1] = {"b2": -twice[1], "R": right, "aR": right * (1.0 / 3.0), "M": 2.0 / (rim[1] * rim[1])}
    k = {i: f[i]["b2"] - f[i - 1]["b2"] for i in range(n)}
    k[-1], k[n] = twice
    u6 = [6.0 * a for a in u]
    g = {i: u6[i] - e[i] for i in range(n)}
    g[-1], g[n] = u6[0], u6[n - 1]
    return finished(f, k, g, n)


def finished(f, k, g, n):
    result = []
    for i in range(n):
        diff, jump = join(
            f[i - 2]["aL"], f[i - 1]["M"], f[i]["R"], k[i - 1],
            f[i + 1]["aR"], f[i]["M"], f[i - 1]["L"], k[i + 1],
            0.5 * k[i],
        )
        result.append(((g[i + 1] - g[i - 1]) + diff, jump))
    return result


def iotas():
    shape = (NV, NY)
    row = lax.broadcasted_iota(jnp.int32, shape, 0)
    lane = lax.broadcasted_iota(jnp.int32, shape, 1)
    return row, lane


def speeds_of(row):
    return speed_low + row.astype(jnp.float32) * np.float32(HV)


def pass_vy(u_ref, v_ref, r_ref, wx_ref, wy_ref, tab_ref, bx_ref, by_ref, pk_ref):
    wide = NHL + 6
    u_rows = u_ref.reshape((NXL + 6) * wide * NV, NY)
    r_rows = v_ref.reshape((NXL + 1) * NHL * NV, NY)

    def speed_terms(x, h, along_x):
        u_at = ((x + 3) * wide + h + 3) * NV
        r_at = (x * NHL + h) * NV
        u_step, r_step = (wide * NV, NHL * NV) if along_x else (NV, NV)
        cells = closed(lambda v: u_rows[pl.ds(u_at + v, 8, stride=u_step), :], NV, EPS_V)
        for v, (total, jump) in enumerate(cells):
            r_rows[pl.ds(r_at + v, 8, stride=r_step), :] = K_V * (jump - jnp.abs(total))

    def y_terms(cells, extra={}):
        row, lane = iotas()
        speeds = speeds_of(row)
        y0, y1 = lane == 0, lane == NY - 1
        for x, h in cells:
            total, jump = along(u_ref[x + 3, h + 3], 1, EPS_X, y0, y1)
            rate = total * (speeds * tab_ref[pl.ds(NHL + h, 1), :] + wy_ref[x])
            if x in extra:
                rate = rate + extra[x]
            if by_ref is not None:
                by_ref[x, h] = jump
            else:
                rate = rate + pk_ref[1] * jump
            r_ref[x, h] = rate

    def middle_terms(h):
        row, _ = iotas()
        lanes = speeds_of(row) * tab_ref[pl.ds(h, 1), :]
        parts = {}
        for i, (total, jump) in enumerate(line(lambda i: u_ref[i + 6, h + 3], 3, EPS_X)):
            parts[3 + i] = total * (lanes + wx_ref[3 + i])
            if bx_ref is not None:
                bx_ref[3 + i, h] = jump
            else:
                parts[3 + i] = parts[3 + i] + pk_ref[0] * jump
        return parts

    def body(t, carry):
        for j in range(3):
            h = 3 * t + j
            parts = middle_terms(h)
            speed_terms(0, h, True)
            y_terms([(x, h) for x in range(8)], parts)
        return carry

    lax.fori_loop(0, NHL // 3, body, 0)
    for x in range(8, NXL):
        for h in (0, NHL - 8):
            speed_terms(x, h, False)
        y_terms([(x, h) for h in range(NHL)])


def pass_h(u_ref, lo, planes, finish):
    def plane(x):
        for h, (total, jump) in enumerate(line(lambda i: u_ref[x + 3, i + 3], NHL, EPS_T)):
            finish(x, h, K_T * (jump - jnp.abs(total)))

    def body(t, carry):
        for j in range(3):
            plane(lo + 3 * t + j)
        return carry

    if planes == 3:
        body(0, 0)
    else:
        lax.fori_loop(0, planes // 3, body, 0)


def pass_x(u_ref, wx_ref, tab_ref, lo, planes, group, finish):
    def body(t, carry):
        row, _ = iotas()
        speeds = speeds_of(row)
        for j in range(group):
            h = t * group + j
            lanes = speeds * tab_ref[pl.ds(h, 1), :]
            cells = line(lambda i: u_ref[lo + i + 3, h + 3], planes, EPS_X)
            for i, (total, jump) in enumerate(cells):
                finish(lo + i, h, total * (lanes + wx_ref[lo + i]), jump)
        return carry

    if group == NHL:
        body(0, 0)
    else:
        lax.fori_loop(0, NHL // group, body, 0)


def bounds():
    speeds = np.float32(speed_low) + np.arange(NV, dtype=np.float32) * np.float32(HV)
    angles = np.arange(NTH, dtype=np.float32) * np.float32(HT)
    px = np.cos(angles)[:, None] * speeds
    py = np.sin(angles)[:, None] * speeds
    return [float(a) for a in (px.max(), -px.min(), py.max(), -py.min())]


def table():
    angles = np.arange(NTH, dtype=np.float32) * np.float32(HT)
    both = np.stack([np.cos(angles).reshape(-1, NHL), np.sin(angles).reshape(-1, NHL)], 1)
    both = both.reshape(NTH // NHL, 2 * NHL, 1).astype(np.float32)
    return np.broadcast_to(both, (NTH // NHL, 2 * NHL, NY)).copy()


def kernel(
    level, wind, mask, depth, tab_all, out,
    u0, u1, u2, r, rv, bx, by, wv, mv, dv, tab, wx, wy, tg, pk, pbuf, pmine,
    sem_in, sx, rx, sh, rh, sp, rp,
):
    g = lax.axis_index("gx")
    hd = lax.axis_index("head")
    ng, nh = lax.axis_size("gx"), lax.axis_size("head")
    yh, z = g // Z, g % Z
    at = lambda half, z_: half * Z + z_
    across = (hd + nh // 2) % nh
    slow = (hd % 8 == 0).astype(jnp.int32)
    helper = (hd % 8 == 1).astype(jnp.int32)
    fields = (u0, u1, u2)

    get_wind = pltpu.make_async_copy(wind, wv, sem_in.at[0])
    get_wind.start()

    barrier = pltpu.get_barrier_semaphore()

    def greet(peer):
        pl.semaphore_signal(barrier, inc=1, device_id=peer, device_id_type=MESH)

    greet({"gx": g, "head": (hd + 1) % nh})
    greet({"gx": g, "head": (hd + nh - 1) % nh})

    @pl.when(g < ng - 1)
    def _():
        greet({"gx": (g + 1) % ng, "head": hd})

    @pl.when(g > 0)
    def _():
        greet({"gx": (g + ng - 1) % ng, "head": hd})

    @pl.when(z == 0)
    def _():
        for i in range(1, Z):
            greet({"gx": at(yh, i), "head": hd + slow})
        for i in range(Z):
            greet({"gx": at(1 - yh, i), "head": across + slow})

    get_level = pltpu.make_async_copy(level, u0.at[pl.ds(3, NXL), pl.ds(3, NHL)], sem_in.at[1])
    get_level.start()
    get_tab = pltpu.make_async_copy(tab_all.at[hd], tab, sem_in.at[2])
    get_tab.start()
    get_mask = pltpu.make_async_copy(mask, mv, sem_in.at[3])
    get_mask.start()
    get_depth = pltpu.make_async_copy(depth, dv, sem_in.at[4])
    get_depth.start()

    get_wind.wait()
    tops = []
    for c in range(2):
        top, low = wv[0, c : c + 1, :], wv[0, c : c + 1, :]
        for i in range(1, NXL):
            top, low = jnp.maximum(top, wv[i, c : c + 1, :]), jnp.minimum(low, wv[i, c : c + 1, :])
        tops += [top, -low]
    row, _ = iotas()
    tile = jnp.broadcast_to(tops[0], (NV, NY))
    for i in range(1, 4):
        tile = jnp.where(row == i, jnp.broadcast_to(tops[i], (NV, NY)), tile)
    pmine[0] = jnp.broadcast_to(jnp.max(tile, axis=1, keepdims=True), (NV, NY))

    def x_copy(s, up, k):
        src = level if s == 0 else fields[s]
        base = 0 if s == 0 else 3
        return pltpu.make_async_remote_copy(
            src_ref=src.at[(NXL - 1 - k if up else k) + base, pl.ds(base, NHL)],
            dst_ref=fields[s].at[2 - k if up else NXL + 3 + k, pl.ds(3, NHL)],
            send_sem=sx.at[s, int(up), k],
            recv_sem=rx.at[s, int(up), k],
            device_id={"gx": (g + 1) % ng if up else (g + ng - 1) % ng, "head": hd},
            device_id_type=MESH,
        )

    def h_copy(s, up, chunk):
        src = level if s == 0 else fields[s]
        base = 0 if s == 0 else 3
        start = (NHL - 3 if up else 0) + base
        return pltpu.make_async_remote_copy(
            src_ref=src.at[pl.ds(3 * chunk + base, 3), pl.ds(start, 3)],
            dst_ref=fields[s].at[pl.ds(3 * chunk + 3, 3), pl.ds(0 if up else NHL + 3, 3)],
            send_sem=sh.at[s, int(up), chunk],
            recv_sem=rh.at[s, int(up), chunk],
            device_id={"gx": g, "head": (hd + 1) % nh if up else (hd + nh - 1) % nh},
            device_id_type=MESH,
        )

    def send_x(s, up):
        @pl.when(g < ng - 1 if up else g > 0)
        def _():
            for k in range(3):
                x_copy(s, up, k).start()

    def take_x(s, up):
        @pl.when(g > 0 if up else g < ng - 1)
        def _():
            for k in range(3):
                x_copy(s, up, k).wait_recv()

        @pl.when(g == 0 if up else g == ng - 1)
        def _():
            for h in range(NHL):
                edge = fields[s][3 if up else NXL + 2, h + 3]
                for i in range(3):
                    fields[s][i if up else NXL + 3 + i, h + 3] = edge

    def send_h(s, chunk):
        for up in (True, False):
            h_copy(s, up, chunk).start()

    def take_h(s, chunk):
        for up in (True, False):
            h_copy(s, up, chunk).wait_recv()

    to_root = lambda back: pltpu.make_async_remote_copy(
        src_ref=pmine.at[0, pl.ds(0, 4)], dst_ref=pbuf.at[z, pl.ds(0, 4)], send_sem=sp.at[(Z + 1) * back], recv_sem=rp.at[z],
        device_id={"gx": at(yh, 0), "head": hd - back}, device_id_type=MESH,
    )
    to_other = lambda back: pltpu.make_async_remote_copy(
        src_ref=pmine.at[0, pl.ds(0, 4)], dst_ref=pbuf.at[Z + z, pl.ds(0, 4)], send_sem=sp.at[1 + (Z + 1) * back],
        recv_sem=rp.at[Z + z], device_id={"gx": at(1 - yh, 0), "head": across - back}, device_id_type=MESH,
    )

    def push(act):
        for back in (0, 1):
            who = helper == 1 if back else slow == 0

            @pl.when(jnp.logical_and(who, z > 0))
            def _():
                act(to_root(back))

            @pl.when(who)
            def _():
                act(to_other(back))

    answer = lambda i: pltpu.make_async_remote_copy(
        src_ref=pmine.at[1, pl.ds(0, 4)], dst_ref=pbuf.at[2 * Z, pl.ds(0, 4)], send_sem=sp.at[1 + i], recv_sem=rp.at[2 * Z],
        device_id={"gx": at(yh, i), "head": hd}, device_id_type=MESH,
    )
    arrived = lambda slot: pltpu.make_async_remote_copy(
        src_ref=pmine.at[0, pl.ds(0, 4)], dst_ref=pbuf.at[slot, pl.ds(0, 4)], send_sem=sp.at[0], recv_sem=rp.at[slot],
        device_id={"gx": at(1 - yh, 0), "head": across}, device_id_type=MESH,
    )

    roots = (1 + (z > 0).astype(jnp.int32)) * (1 + helper - slow)
    greeters = 2 + (g > 0).astype(jnp.int32) + (g < ng - 1).astype(jnp.int32) + roots
    pl.semaphore_wait(barrier, greeters)

    push(lambda copy: copy.start())
    send_x(0, True)
    send_x(0, False)
    for chunk in range(3):
        send_h(0, chunk)

    for i in range(NXL):
        wx[i] = jnp.broadcast_to(wv[i, 0:1, :], (NV, NY))
        wy[i] = jnp.broadcast_to(wv[i, 1:2, :], (NV, NY))
    get_mask.wait()
    get_depth.wait()
    for i in range(NXL):
        d = dv[i : i + 1, :]
        tg[i] = jnp.broadcast_to(jnp.where(mv[i : i + 1, :] == 1, -d, d), (NV, NY))
    get_tab.wait()
    get_level.wait()

    pass_vy(u0, rv, r, wx, wy, tab, bx, by, None)
    for chunk in range(3):
        take_h(0, chunk)
    def add(x, h, part):
        r[x, h] = (r[x, h] + rv[x, h]) + part

    pass_h(u0, 0, NXL, add)

    def keep(x, h, part, jump):
        r[x, h] = r[x, h] + part
        bx[x, h] = jump

    def either(low, first, second):
        pl.when(low)(first)
        pl.when(jnp.logical_not(low))(second)

    def both_sides(s, finish, after):
        turned = jnp.logical_or(g == Z, g == Z - 1)

        def body(j, carry):
            low = jnp.logical_xor(j == 0, turned)
            high = jnp.logical_not(low)
            seam = jnp.logical_and(s > 0, jnp.logical_and(turned, low == (g == Z)))
            plain = jnp.logical_not(seam)
            if s > 0:
                either(low, lambda: take_h(s, 0), lambda: take_h(s, 2))
                pass_h(fields[s], jnp.where(low, 0, 6), 3, add)
            pl.when(jnp.logical_and(plain, low))(lambda: take_x(s, True))
            pl.when(jnp.logical_and(plain, high))(lambda: take_x(s, False))

            @pl.when(plain)
            def _():
                pass_x(fields[s], wx, tab, jnp.where(low, 0, 6), 3, NHL, finish)

            if s == 1:
                pl.when(jnp.logical_and(plain, low))(lambda: send_x(2, False))
                pl.when(jnp.logical_and(plain, high))(lambda: send_x(2, True))
            if s > 0:

                @pl.when(seam)
                def _():
                    for k in range(3):
                        either(low, lambda: x_copy(s, True, k).wait_recv(), lambda: x_copy(s, False, k).wait_recv())
                        pass_x(fields[s], wx, tab, jnp.where(low, 2 - k, 6 + k), 1, NHL, finish)
                        if s == 1:
                            either(low, lambda: x_copy(2, False, 2 - k).start(), lambda: x_copy(2, True, 2 - k).start())

            either(low, lambda: after(0), lambda: after(2))
            return carry

        lax.fori_loop(0, 2, body, 0)

    both_sides(0, keep, lambda chunk: None)

    @pl.when(z == 0)
    def _():
        best = pmine[0, 0:4]
        for slot in range(1, 2 * Z):
            arrived(slot).wait_recv()
            best = jnp.maximum(best, pbuf[slot, 0:4])
        pmine[1, 0:4] = best
        for i in (Z - 1, *range(1, Z - 1)):
            answer(i).start()

    @pl.when(z > 0)
    def _():
        arrived(2 * Z).wait_recv()
        pmine[1, 0:4] = pbuf[2 * Z, 0:4]

    top = pmine[1, 0:4]
    cx, cnx, cy, cny = bounds()
    peak_x = jnp.maximum(top[0:1] + cx, top[1:2] + cnx)
    peak_y = jnp.maximum(top[2:3] + cy, top[3:4] + cny)
    step = courant / (peak_x / spacing + peak_y / spacing + turn_limit / HT + thrust_limit / HV)
    pk[0] = jnp.broadcast_to(peak_x, (NV, NY))
    pk[1] = jnp.broadcast_to(peak_y, (NV, NY))
    pk[2] = jnp.broadcast_to(step * (1.0 / (12.0 * spacing)), (NV, NY))

    def update_one(lo):
        def body(h, carry):
            px, py, dt = pk[0], pk[1], pk[2]
            for i in range(3):
                rate = r[lo + i, h] + px * bx[lo + i, h] + py * by[lo + i, h]
                u1[lo + i + 3, h + 3] = jnp.minimum(u0[lo + i + 3, h + 3] + dt * rate, tg[lo + i])
            return carry

        lax.fori_loop(0, NHL, body, 0, unroll=2)

    update_one(0)
    send_x(1, False)
    send_h(1, 0)
    update_one(6)
    send_x(1, True)
    send_h(1, 2)
    update_one(3)
    send_h(1, 1)

    def section(s, write, after):
        u = fields[s]
        old, new = (0.75, 0.25) if s == 1 else (1.0 / 3.0, 2.0 / 3.0)
        pass_vy(u, rv, r, wx, wy, tab, None, None, pk)

        def close(x, h, rate):
            now = old * u0[x + 3, h + 3] + new * (u[x + 3, h + 3] + pk[2] * rate)
            write(x, h, jnp.minimum(now, tg[x]))

        def finish_x(x, h, part, jump):
            close(x, h, (r[x, h] + part) + pk[0] * jump)

        def finish_h(x, h, part):
            close(x, h, (r[x, h] + rv[x, h]) + part)

        def middle():
            take_h(s, 1)
            pass_h(u, 3, 3, finish_h)
            after(1)

        if s == 2:
            middle()
        else:
            pl.when(g == Z)(middle)
        both_sides(s, finish_x, after)
        if s == 1:
            pl.when(g != Z)(middle)

    def write_two(x, h, value):
        u2[x + 3, h + 3] = value

    section(1, write_two, lambda chunk: send_h(2, chunk))

    def write_out(x, h, value):
        out[x, h] = value

    section(2, write_out, lambda chunk: None)


    push(lambda copy: copy.wait_send())

    @pl.when(z == 0)
    def _():
        for i in range(1, Z):
            answer(i).wait_send()

    for s in range(3):
        for up in (True, False):

            @pl.when(g < ng - 1 if up else g > 0)
            def _():
                for k in range(3):
                    x_copy(s, up, k).wait_send()

            for chunk in range(3):
                h_copy(s, up, chunk).wait_send()


def local(level_set, wind_field, target_mask, target_depth):
    field = pltpu.VMEM((NXL + 6, NHL + 6, NV, NY), jnp.float32)
    inner = pltpu.VMEM((NXL, NHL, NV, NY), jnp.float32)
    rows = pltpu.VMEM((NXL, NV, NY), jnp.float32)
    dma = pltpu.SemaphoreType.DMA
    inputs = (level_set, jnp.transpose(wind_field, (1, 0, 2)), target_mask, target_depth, jnp.asarray(table()))
    return pl.pallas_call(
        kernel,
        out_shape=jax.ShapeDtypeStruct(level_set.shape, jnp.float32),
        in_specs=[pl.BlockSpec(memory_space=pltpu.HBM)] * 5,
        out_specs=pl.BlockSpec(memory_space=pltpu.VMEM),
        scratch_shapes=[
            field, field, field, inner, pltpu.VMEM((NXL + 1, NHL, NV, NY), jnp.float32), inner, inner,
            pltpu.VMEM((NXL, 2, NY), jnp.float32),
            pltpu.VMEM((NXL, NY), jnp.int32),
            pltpu.VMEM((NXL, NY), jnp.float32),
            pltpu.VMEM((2 * NHL, NY), jnp.float32),
            rows, rows, rows,
            pltpu.VMEM((3, NV, NY), jnp.float32),
            pltpu.VMEM((2 * Z + 1, NV, NY), jnp.float32),
            pltpu.VMEM((2, NV, NY), jnp.float32),
            dma((5,)), dma((3, 2, 3)), dma((3, 2, 3)), dma((3, 2, 3)), dma((3, 2, 3)), dma((Z + 3,)), dma((2 * Z + 1,)),
        ],
        compiler_params=pltpu.CompilerParams(collective_id=0, has_side_effects=True, vmem_limit_bytes=32 * 1024 * 1024),
        name="step",
    )(*[pltpu.with_memory_space_constraint(a, pltpu.HBM) for a in inputs])


def solution(mesh):
    return jax.shard_map(
        local,
        mesh=mesh,
        in_specs=(P("gx", "head", None, None), P(None, "gx", None), P("gx", None), P("gx", None)),
        out_specs=P("gx", "head", None, None),
        check_vma=False,
    )
```
